128 devices in a mesh: seq: 4 (over z), exp: 32 (over y, x, core).
Axes of the slice: x: 4, y: 4, z: 4, core: 2. Of those that a mesh axis runs over, the one named last changes fastest.
Arguments:
- streams: bfloat16 [8192, 4, 3584], P(('seq', 'exp')), may hold values from -6 to 6
- phi_matrix: bfloat16 [24, 14336], replicated, may hold values from -0.046875 to 0.046875
- mix_scale: float32 [3], replicated, may hold values from 0.5 to 2
- mix_bias: float32 [24], replicated, may hold values from -1 to 1
- router: bfloat16 [32, 3584], replicated, may hold values from -0.09375 to 0.09375
- expert_index_table: int32 [8192, 8], P(('seq', 'exp')), may hold values from 0 to 31, all different within a row; in each aligned block of 64 rows (0 to 63, 64 to 127, ...) at most 20 rows name the same one
- w_gate: bfloat16 [32, 3584, 2048], P('exp', None, 'seq'), may hold values from -0.09375 to 0.09375
- w_up: bfloat16 [32, 3584, 2048], P('exp', None, 'seq'), may hold values from -0.09375 to 0.09375
- down_weight: bfloat16 [32, 2048, 3584], P('exp', 'seq'), may hold values from -0.125 to 0.125
Outputs:
- new_streams: bfloat16 [8192, 4, 3584], P(('seq', 'exp'))
The draws below stay inside these ranges and needn't reach their ends.
Inputs may be any that keep to these rules, and one draw needn't show every extreme that they name: `expert_index_table`: each row names 8 different experts; among the 64 rows of one device (aligned blocks of 64 rows) no expert is named by more than 20 rows, a bound that some block reaches; every expert is named somewhere.
All inputs are finite; a program needn't handle non-finite values.
Results may differ from the reference program's by a relative error of at most 0.012.
Values may be sent and summed in bfloat16 or wider, within the bound.
No kernel may reach another device: no remote copies, remote signals or barrier semaphores. Data moves between devices by JAX's collectives and lax.ppermute only.
A program may use at most 192 MiB of HBM per device.

```python
import math
import jax
import jax.numpy as jnp
import numpy as np
from jax import lax

D = 3584
FF = 2048
STREAMS = 4
TOPK = 8
BALANCE_SWEEPS = 20
EXPERTS = 32
TOK_DEV = 64
TOKENS = 8192
CAP = 20
MIXES = 24
N_SEQ = 4
N_EXP = 32


def shard_levels(rng, dims, pieces, low, top_value):
    gain, own = 1.0, jax.random.fold_in(rng, 6)
    for axis_at, shards_of in pieces:
        draws = jnp.exp(jax.random.uniform(jax.random.fold_in(own, axis_at), (shards_of,), jnp.float32, low / len(pieces), top_value / len(pieces)))
        gain = gain * jnp.repeat(draws, dims[axis_at] // shards_of).reshape([-1 if axis == axis_at else 1 for axis in range(len(dims))])
    return gain


def deal_out(rng, own, number, rows, amount, top, most, slope):
    sequence = jax.random.permutation(rng, amount)
    crowded, ordinary = load_shares(amount, rows * top, most, slope, True), load_shares(amount, rows * top, most, slope, False)
    places = jnp.arange(amount)

    def named(lengths, offset_by):
        used = int((lengths > 0).sum())
        fixed = max(1, used // 4)
        shifted = fixed + (places - fixed + offset_by * (used - fixed)) % max(1, amount - fixed)
        return jnp.zeros((amount,), jnp.int32).at[sequence[jnp.where(places < fixed, places, shifted)]].set(jnp.asarray(lengths, jnp.int32))

    lengths = jnp.where(number % 4 == 0, named(crowded, number // 4), named(ordinary, number - number // 4 - 1))
    mixed = jax.random.permutation(jax.random.fold_in(own, 3), amount)
    donor, taker = mixed[0:amount // 2 * 2:2], mixed[1:amount // 2 * 2:2]
    margin = jnp.minimum(lengths[donor] - 1, most - lengths[taker]) // 2
    margin = jnp.where((donor == sequence[0]) | (taker == sequence[0]) | (lengths[taker] == 0), 0, jnp.maximum(margin, 0))
    shifted = jax.random.randint(jax.random.fold_in(own, 4), (amount // 2,), 0, 1 << 20) % (margin + 1)
    lengths = lengths.at[donor].add(-shifted).at[taker].add(shifted)
    members = jnp.searchsorted(jnp.cumsum(lengths), jnp.arange(rows * top), side="right").astype(jnp.int32)
    listing = members.reshape(top, rows).T
    listing = listing[jax.random.permutation(jax.random.fold_in(own, 1), rows)]
    offset_by = jax.random.randint(jax.random.fold_in(own, 2), (rows, 1), 0, top)
    return jnp.take_along_axis(listing, (jnp.arange(top)[None, :] + offset_by) % top, axis=1)


def load_shares(number_of, total, most, skew, full):
    portions = [(1 << 20) // math.isqrt(grade ** skew) + 1 for grade in range(1, number_of + 1)]
    largest = most if full else min(most, max(-(-total // number_of), total * portions[0] // sum(portions)))
    least = 1 if total - largest >= number_of - 1 else 0
    holding, surplus = [largest] + [least] * (number_of - 1), total - largest - least * (number_of - 1)
    while surplus > 0:
        movable = [i for i in range(1, number_of) if holding[i] < largest] or [i for i in range(1, number_of) if holding[i] < most]
        pool, remaining = sum([portions[i] for i in movable]), surplus
        for i in movable:
            extra = min(most - holding[i], max(1, remaining * portions[i] // pool), surplus)
            holding[i] = holding[i] + extra
            surplus = surplus - extra
    return np.array(holding)


def bell_draw(rng, dims, scale, reach, cuts=(), kind=jnp.bfloat16):
    array = scale * jax.random.normal(rng, dims, jnp.float32)
    if cuts:
        array = array * shard_levels(rng, dims, cuts, -0.22, 0.18)
    return jnp.clip(array, -reach, reach).astype(kind)


def setup_inputs(seed: int = 0) -> dict:
    arg_keys = jax.random.split(jax.random.key(seed), 10)
    streams = bell_draw(arg_keys[0], (TOKENS, STREAMS, D), 1.0, 6.0, ((0, 128),))
    phi_matrix = bell_draw(arg_keys[1], (MIXES, STREAMS * D), (STREAMS * D) ** -0.5, 0.046875)
    mix_scale = jnp.clip(jnp.exp(jax.random.uniform(arg_keys[2], (3,), jnp.float32, math.log(0.5), math.log(2.0))), 0.5, 2.0)
    mix_bias = jnp.clip(jax.random.uniform(arg_keys[3], (MIXES,), jnp.float32, -1.0, 1.0), -1.0, 1.0)
    router = bell_draw(arg_keys[4], (EXPERTS, D), D ** -0.5, 0.09375)
    expert_index_table_keys = jax.random.split(jax.random.fold_in(arg_keys[5], 1), TOKENS // TOK_DEV)
    expert_index_table_turns = jax.random.permutation(jax.random.fold_in(arg_keys[5], 3), TOKENS // TOK_DEV)
    expert_index_table = jax.vmap(lambda own, number: deal_out(jax.random.fold_in(arg_keys[5], 2), own, number, TOK_DEV, EXPERTS, TOPK, CAP, 2))(expert_index_table_keys, expert_index_table_turns).reshape((TOKENS, TOPK))
    w_gate = bell_draw(arg_keys[6], (EXPERTS, D, FF), D ** -0.5, 0.09375, ((0, 32), (2, 4)))
    w_up = bell_draw(arg_keys[7], (EXPERTS, D, FF), D ** -0.5, 0.09375, ((0, 32), (2, 4)))
    down_weight = bell_draw(arg_keys[8], (EXPERTS, FF, D), FF ** -0.5, 0.125, ((0, 32), (1, 4)))
    return dict(streams=streams, phi_matrix=phi_matrix, mix_scale=mix_scale, mix_bias=mix_bias, router=router, expert_index_table=expert_index_table, w_gate=w_gate, w_up=w_up, down_weight=down_weight)


def mix_coefficients(streams, phi_matrix, mix_scale, mix_bias):
    count = streams.shape[1]
    flat = streams.astype(jnp.float32).reshape(streams.shape[0], -1)
    normed = flat * lax.rsqrt(lax.optimization_barrier(jnp.mean(flat * flat, axis=1, keepdims=True)) + 1e-06)
    normed = normed.astype(jnp.bfloat16)
    coeffs = lax.dot_general(normed, phi_matrix, (((1,), (1,)), ((), ())), preferred_element_type=jnp.float32)
    pre = jax.nn.sigmoid(mix_scale[0] * coeffs[:, :count] + mix_bias[:count])
    post = 2.0 * jax.nn.sigmoid(mix_scale[1] * coeffs[:, count:2 * count] + mix_bias[count:2 * count])
    logits = mix_scale[2] * coeffs[:, 2 * count:] + mix_bias[2 * count:]
    mixing = jnp.exp(logits).reshape(-1, count, count)
    for sweep_step in range(BALANCE_SWEEPS):
        mixing = mixing / lax.optimization_barrier(jnp.sum(mixing, axis=2, keepdims=True))
        mixing = mixing / lax.optimization_barrier(jnp.sum(mixing, axis=1, keepdims=True))
    return (pre, post, mixing)

def mix_input(streams, pre):
    total = pre[:, 0, None] * streams[:, 0, :].astype(jnp.float32)
    for stream in range(1, streams.shape[1]):
        total = total + pre[:, stream, None] * streams[:, stream, :].astype(jnp.float32)
    return total.astype(jnp.bfloat16)

def mix_output(streams, mixing, post, moe_out):
    rows = []
    for target in range(streams.shape[1]):
        total = mixing[:, target, 0, None] * streams[:, 0, :].astype(jnp.float32)
        for source in range(1, streams.shape[1]):
            total = total + mixing[:, target, source, None] * streams[:, source, :].astype(jnp.float32)
        rows.append(total + post[:, target, None] * moe_out)
    return jnp.stack(rows, axis=1).astype(jnp.bfloat16)

def route_gates(layer_in, router, expert_index_table):
    logits = lax.dot_general(layer_in, router, (((1,), (1,)), ((), ())), preferred_element_type=jnp.float32)
    affinity = jax.nn.sigmoid(logits)
    chosen = jnp.take_along_axis(affinity, expert_index_table, axis=1)
    return 2.5 * chosen / lax.optimization_barrier(jnp.sum(chosen, axis=1, keepdims=True))

def reference(streams, phi_matrix, mix_scale, mix_bias, router, expert_index_table, w_gate, w_up, down_weight):
    pre, post, mixing = mix_coefficients(streams, phi_matrix, mix_scale, mix_bias)
    layer_in = mix_input(streams, pre)
    gates = route_gates(layer_in, router, expert_index_table)
    limit = N_SEQ * N_EXP * CAP
    group_width = FF // N_SEQ
    width = streams.shape[2]

    def one_expert(total, inputs):
        weight_gate, weight_up, weight_down, expert = inputs
        hits = expert_index_table == expert
        chosen = jnp.any(hits, axis=1)
        weight = lax.optimization_barrier(jnp.sum(jnp.where(hits, gates, 0.0), axis=1))
        index = jnp.nonzero(chosen, size=limit, fill_value=0)[0].astype(jnp.int32)
        valid = (jnp.arange(limit) < jnp.sum(chosen.astype(jnp.int32))).astype(jnp.float32)
        rows = layer_in[index]
        gate_part = jnp.dot(rows, weight_gate, preferred_element_type=jnp.float32)
        up_part = jnp.dot(rows, weight_up, preferred_element_type=jnp.float32)
        hidden = (jax.nn.silu(gate_part) * up_part).astype(jnp.bfloat16)
        output = jnp.zeros((limit, width), jnp.float32)
        for group in range(N_SEQ):
            part = jnp.dot(hidden[:, group * group_width:(group + 1) * group_width], weight_down[group * group_width:(group + 1) * group_width], preferred_element_type=jnp.float32).astype(jnp.bfloat16)
            part = lax.optimization_barrier(part)
            output = output + part.astype(jnp.float32)
        total = total.at[index].add((weight[index] * valid)[:, None] * output)
        return (total, None)
    experts = jnp.arange(EXPERTS, dtype=jnp.int32)
    moe_out, ignored_entry = lax.scan(one_expert, jnp.zeros((streams.shape[0], width), jnp.float32), (w_gate, w_up, down_weight, experts))
    return mix_output(streams, mixing, post, moe_out)
```

```python
import functools

import jax
import jax.numpy as jnp
from jax import lax
from jax.experimental import pallas as pl
from jax.experimental.pallas import tpu as pltpu
from jax.sharding import Mesh, PartitionSpec as P

BALANCE_SWEEPS = 20
EXPERTS = 32
CAP = 20
TOK = 64
GROUP = 256
SLOTS = GROUP // TOK * CAP
PER_STEP = 2
GATE_LANES = 128
RING = 4


def mix_coefficients(streams, phi_matrix, mix_scale, mix_bias):
    count = streams.shape[1]
    flat = streams.astype(jnp.float32).reshape(streams.shape[0], -1)
    normed = flat * lax.rsqrt(jnp.mean(flat * flat, axis=1, keepdims=True) + 1e-06)
    normed = normed.astype(jnp.bfloat16)
    coeffs = lax.dot_general(
        normed, phi_matrix, (((1,), (1,)), ((), ())), preferred_element_type=jnp.float32
    )
    pre = jax.nn.sigmoid(mix_scale[0] * coeffs[:, :count] + mix_bias[:count])
    post = 2.0 * jax.nn.sigmoid(
        mix_scale[1] * coeffs[:, count : 2 * count] + mix_bias[count : 2 * count]
    )
    logits = mix_scale[2] * coeffs[:, 2 * count :] + mix_bias[2 * count :]
    mixing = jnp.exp(logits).reshape(-1, count, count)
    for sweep_step in range(BALANCE_SWEEPS):
        mixing = mixing / jnp.sum(mixing, axis=2, keepdims=True)
        mixing = mixing / jnp.sum(mixing, axis=1, keepdims=True)
    return (pre, post, mixing)


def mix_input(streams, pre):
    total = pre[:, 0, None] * streams[:, 0, :].astype(jnp.float32)
    for stream in range(1, streams.shape[1]):
        total = total + pre[:, stream, None] * streams[:, stream, :].astype(jnp.float32)
    return total.astype(jnp.bfloat16)


def mix_output(streams, mixing, post, moe_out):
    rows = []
    for target in range(streams.shape[1]):
        total = mixing[:, target, 0, None] * streams[:, 0, :].astype(jnp.float32)
        for source in range(1, streams.shape[1]):
            total = total + mixing[:, target, source, None] * streams[:, source, :].astype(
                jnp.float32
            )
        rows.append(total + post[:, target, None] * moe_out)
    return jnp.stack(rows, axis=1).astype(jnp.bfloat16)


def dense_gates(layer_in, router, expert_index_table):
    logits = lax.dot_general(
        layer_in, router, (((1,), (1,)), ((), ())), preferred_element_type=jnp.float32
    )
    affinity = jax.nn.sigmoid(logits)
    experts = lax.iota(jnp.int32, EXPERTS)
    named = jnp.any(expert_index_table[:, :, None] == experts[None, None, :], axis=1)
    chosen = jnp.where(named, affinity, 0.0)
    gates = 2.5 * chosen / jnp.sum(chosen, axis=1, keepdims=True)
    high = lax.reduce_precision(gates, 8, 7)
    low = gates - high
    pad = jnp.zeros((gates.shape[0], GATE_LANES - 2 * EXPERTS), jnp.float32)
    return jnp.concatenate([high, low, pad], axis=1).astype(jnp.bfloat16)


def expert_kernel(
    ids, x_ref, wg0, wu0, wd0, wg1, wu1, wd1, o_ref, st_ref, gate_ref, rows_ref, y_ref
):
    width = o_ref.shape[-1]
    tile = min(512, width)
    lane = lax.broadcasted_iota(jnp.int32, (GROUP, GATE_LANES), 1)
    row = lax.broadcasted_iota(jnp.int32, (GROUP, GROUP), 0)
    col = lax.broadcasted_iota(jnp.int32, (GROUP, GROUP), 1)
    before = ((col < row) & (col // TOK == row // TOK)).astype(jnp.float32).astype(jnp.bfloat16)
    block = lax.broadcasted_iota(jnp.int32, (GROUP, 1), 0) // TOK
    slot_of = lax.broadcasted_iota(jnp.int32, (GROUP, 2 * SLOTS), 1)
    slot_lane = lax.broadcasted_iota(jnp.int32, (SLOTS, GATE_LANES), 1)
    for g in range(PER_STEP):
        rows = pl.ds(g * GROUP, GROUP)
        gates = x_ref[rows, width : width + GATE_LANES]
        hit = (gates.astype(jnp.float32) != 0.0).astype(jnp.float32)
        rank = jnp.dot(before, hit.astype(jnp.bfloat16), preferred_element_type=jnp.float32)
        slots = []
        for e in range(2):
            mine = lane == ids[e]
            rank_e = jnp.sum(jnp.where(mine, rank, 0.0), axis=1, keepdims=True)
            hit_e = jnp.sum(jnp.where(mine, hit, 0.0), axis=1, keepdims=True)
            place = rank_e.astype(jnp.int32) + block * CAP + e * SLOTS
            slots.append(jnp.where(hit_e > 0.0, place, -1))
        st = (slot_of == slots[0]) | (slot_of == slots[1])
        st_ref[g] = st.astype(jnp.float32).astype(jnp.bfloat16)
        picked = lax.dot_general(
            st_ref[g], gates, (((0,), (0,)), ((), ())), preferred_element_type=jnp.float32
        )
        for e in range(2):
            own = picked[e * SLOTS : (e + 1) * SLOTS]
            wanted = (slot_lane == ids[e]) | (slot_lane == ids[e] + EXPERTS)
            gate_ref[e, pl.ds(g * SLOTS, SLOTS), :] = jnp.broadcast_to(
                jnp.sum(jnp.where(wanted, own, 0.0), axis=1, keepdims=True), (SLOTS, GATE_LANES)
            )

        @pl.loop(0, width // tile)
        def _(n):
            cols = pl.ds(pl.multiple_of(n * tile, tile), tile)
            rows_ref[g, :, cols] = lax.dot_general(
                st_ref[g],
                x_ref[rows, cols],
                (((0,), (0,)), ((), ())),
                preferred_element_type=jnp.float32,
            ).astype(jnp.bfloat16)

    for e, (wg, wu, wd) in enumerate(((wg0, wu0, wd0), (wg1, wu1, wd1))):
        mine = slice(e * SLOTS, (e + 1) * SLOTS)
        xs = jnp.concatenate([rows_ref[g, mine, :] for g in range(PER_STEP)], axis=0)
        gate_part = jnp.dot(xs, wg[...], preferred_element_type=jnp.float32)
        up_part = jnp.dot(xs, wu[...], preferred_element_type=jnp.float32)
        hidden = gate_part / (1.0 + jnp.exp(-gate_part)) * up_part
        hidden = (hidden * gate_ref[e, :, 0:1]).astype(jnp.bfloat16)

        @pl.loop(0, width // tile)
        def _(n):
            cols = pl.ds(pl.multiple_of(n * tile, tile), tile)
            part = jnp.dot(hidden, wd[:, cols], preferred_element_type=jnp.float32)
            part = part.astype(jnp.bfloat16)
            for g in range(PER_STEP):
                y_ref[g, mine, cols] = part[g * SLOTS : (g + 1) * SLOTS]

    for g in range(PER_STEP):

        @pl.loop(0, width // tile)
        def _(n):
            cols = pl.ds(pl.multiple_of(n * tile, tile), tile)
            out = jnp.dot(st_ref[g], y_ref[g, :, cols], preferred_element_type=jnp.float32)
            out = out.astype(jnp.bfloat16)
            for b in range(GROUP // TOK):
                o_ref[g * (GROUP // TOK) + b, 0, :, cols] = out[b * TOK : (b + 1) * TOK]


def expert_call(ids, gathered, weights, width, ff):
    tokens = gathered.shape[0]
    step = PER_STEP * GROUP
    steps = tokens // step
    planes = RING
    per_plane = steps // planes
    chips = tokens // TOK // planes
    rows = PER_STEP * SLOTS
    whole = lambda shape: pl.BlockSpec(
        shape, lambda i, ids: (0, 0), pipeline_mode=pl.Buffered(1)
    )
    up, down = whole((width, ff)), whole((ff, width))
    return pl.pallas_call(
        expert_kernel,
        out_shape=jax.ShapeDtypeStruct((chips, planes, TOK, width), jnp.bfloat16),
        grid_spec=pltpu.PrefetchScalarGridSpec(
            num_scalar_prefetch=1,
            grid=(steps,),
            in_specs=[
                pl.BlockSpec((step, width + GATE_LANES), lambda i, ids: (i, 0)),
                up, up, down, up, up, down,
            ],
            out_specs=pl.BlockSpec(
                (step // TOK, 1, TOK, width),
                lambda i, ids: (i % per_plane, i // per_plane, 0, 0),
            ),
            scratch_shapes=[
                pltpu.VMEM((PER_STEP, GROUP, 2 * SLOTS), jnp.bfloat16),
                pltpu.VMEM((2, rows, GATE_LANES), jnp.float32),
                pltpu.VMEM((PER_STEP, 2 * SLOTS, width), jnp.bfloat16),
                pltpu.VMEM((PER_STEP, 2 * SLOTS, width), jnp.bfloat16),
            ],
        ),
        compiler_params=pltpu.CompilerParams(
            dimension_semantics=("arbitrary",), vmem_limit_bytes=58 << 20
        ),
        cost_estimate=pl.CostEstimate(
            flops=12 * steps * rows * width * ff,
            bytes_accessed=4 * tokens * width,
            transcendentals=0,
        ),
        name="experts",
    )(ids, gathered, *weights)


def body(
    streams, phi_matrix, mix_scale, mix_bias, router, expert_index_table, w_gate, w_up, down_weight
):
    width, ff = w_gate.shape[1], w_gate.shape[2]
    swap = [(0, 1), (1, 0)]
    own = (w_gate[0], w_up[0], down_weight[0])
    other = tuple(lax.ppermute(w, "c", swap) for w in own)
    pre, post, mixing = mix_coefficients(streams, phi_matrix, mix_scale, mix_bias)
    layer_in = mix_input(streams, pre)
    gates = dense_gates(layer_in, router, expert_index_table)
    packed = jnp.concatenate([layer_in, gates], axis=1)
    gathered = lax.all_gather(packed, ("z", "y", "x"), axis=0, tiled=True)
    core = lax.axis_index("c")
    pair = 2 * (lax.axis_index("y") * RING + lax.axis_index("x"))
    ids = jnp.stack([pair + core, pair + 1 - core]).astype(jnp.int32)
    dense = expert_call(ids, gathered, own + other, width, ff)
    summed = lax.psum_scatter(
        dense.reshape(-1, width), ("y", "x"), scatter_dimension=0, tiled=True
    ).reshape(RING, TOK, width)
    plane = lax.axis_index("z")
    moe_out = lax.dynamic_index_in_dim(summed, plane, 0, keepdims=False).astype(jnp.float32)
    for shift in range(1, RING):
        away = lax.dynamic_index_in_dim(summed, (plane + shift) % RING, 0, keepdims=False)
        ring = [(i, (i + shift) % RING) for i in range(RING)]
        moe_out = moe_out + lax.ppermute(away, "z", ring).astype(jnp.float32)
    return mix_output(streams, mixing, post, moe_out)


def solution(mesh):
    torus = Mesh(mesh.devices.reshape(RING, RING, RING, 2), ("z", "y", "x", "c"))
    tokens, experts = ("z", "y", "x", "c"), ("y", "x", "c")
    in_specs = (
        P(tokens, None, None),
        P(),
        P(),
        P(),
        P(),
        P(tokens, None),
        P(experts, None, "z"),
        P(experts, None, "z"),
        P(experts, "z", None),
    )
    out_specs = P(tokens, None, None)
    return jax.shard_map(
        body, mesh=torus, in_specs=in_specs, out_specs=out_specs, check_vma=False
    )
```

```python
import functools

import jax
import jax.numpy as jnp
from jax import lax
from jax.experimental import pallas as pl
from jax.experimental.pallas import tpu as pltpu
from jax.sharding import Mesh, PartitionSpec as P

BALANCE_SWEEPS = 20
EXPERTS = 32
CAP = 20
TOK = 64
GROUP = 256
SLOTS = GROUP // TOK * CAP
GATE_LANES = 128
RING = 4
PLANE_COLS = 1280


def mix_coefficients(streams, phi_matrix, mix_scale, mix_bias):
    count = streams.shape[1]
    flat = streams.astype(jnp.float32).reshape(streams.shape[0], -1)
    normed = flat * lax.rsqrt(jnp.mean(flat * flat, axis=1, keepdims=True) + 1e-06)
    normed = normed.astype(jnp.bfloat16)
    coeffs = lax.dot_general(
        normed, phi_matrix, (((1,), (1,)), ((), ())), preferred_element_type=jnp.float32
    )
    pre = jax.nn.sigmoid(mix_scale[0] * coeffs[:, :count] + mix_bias[:count])
    post = 2.0 * jax.nn.sigmoid(
        mix_scale[1] * coeffs[:, count : 2 * count] + mix_bias[count : 2 * count]
    )
    logits = mix_scale[2] * coeffs[:, 2 * count :] + mix_bias[2 * count :]
    mixing = jnp.exp(logits).reshape(-1, count, count)
    for sweep_step in range(BALANCE_SWEEPS):
        mixing = mixing / jnp.sum(mixing, axis=2, keepdims=True)
        mixing = mixing / jnp.sum(mixing, axis=1, keepdims=True)
    return (pre, post, mixing)


def mix_input(streams, pre):
    total = pre[:, 0, None] * streams[:, 0, :].astype(jnp.float32)
    for stream in range(1, streams.shape[1]):
        total = total + pre[:, stream, None] * streams[:, stream, :].astype(jnp.float32)
    return total.astype(jnp.bfloat16)


def mix_output(streams, mixing, post, moe_out):
    rows = []
    for target in range(streams.shape[1]):
        total = mixing[:, target, 0, None] * streams[:, 0, :].astype(jnp.float32)
        for source in range(1, streams.shape[1]):
            total = total + mixing[:, target, source, None] * streams[:, source, :].astype(
                jnp.float32
            )
        rows.append(total + post[:, target, None] * moe_out)
    return jnp.stack(rows, axis=1).astype(jnp.bfloat16)


def dense_gates(layer_in, router, expert_index_table):
    logits = lax.dot_general(
        layer_in, router, (((1,), (1,)), ((), ())), preferred_element_type=jnp.float32
    )
    affinity = jax.nn.sigmoid(logits)
    experts = lax.iota(jnp.int32, EXPERTS)
    named = jnp.any(expert_index_table[:, :, None] == experts[None, None, :], axis=1)
    chosen = jnp.where(named, affinity, 0.0)
    gates = 2.5 * chosen / jnp.sum(chosen, axis=1, keepdims=True)
    high = lax.reduce_precision(gates, 8, 7)
    low = gates - high
    pad = jnp.zeros((gates.shape[0], GATE_LANES - 2 * EXPERTS), jnp.float32)
    return jnp.concatenate([high, low, pad], axis=1).astype(jnp.bfloat16)


def slots_of_group(ids, gates, before):
    lane = lax.broadcasted_iota(jnp.int32, (GROUP, GATE_LANES), 1)
    block = lax.broadcasted_iota(jnp.int32, (GROUP, 1), 0) // TOK
    slot_of = lax.broadcasted_iota(jnp.int32, (GROUP, GROUP), 1)
    hit = (gates.astype(jnp.float32) != 0.0).astype(jnp.float32)
    rank = jnp.dot(before, hit.astype(jnp.bfloat16), preferred_element_type=jnp.float32)
    slots = []
    for e in range(2):
        mine = lane == ids[e]
        rank_e = jnp.sum(jnp.where(mine, rank, 0.0), axis=1, keepdims=True)
        hit_e = jnp.sum(jnp.where(mine, hit, 0.0), axis=1, keepdims=True)
        place = rank_e.astype(jnp.int32) + block * CAP + e * SLOTS
        slots.append(jnp.where(hit_e > 0.0, place, -1))
    return ((slot_of == slots[0]) | (slot_of == slots[1])).astype(jnp.float32)


def hidden_kernel(
    ids, gates_ref, x_ref, wg0, wu0, wg1, wu1, hid_ref, st_ref, pick_ref, gate_ref, rows_ref, acc_ref
):
    step, steps = pl.program_id(0), pl.num_programs(0)
    groups = gates_ref.shape[0] // GROUP
    chunk = rows_ref.shape[1] // 4

    @pl.when(step == 0)
    def _():
        acc_ref[...] = jnp.zeros_like(acc_ref)
        row = lax.broadcasted_iota(jnp.int32, (GROUP, GROUP), 0)
        col = lax.broadcasted_iota(jnp.int32, (GROUP, GROUP), 1)
        before = (col < row) & (col // TOK == row // TOK)
        before = before.astype(jnp.float32).astype(jnp.bfloat16)
        slot_lane = lax.broadcasted_iota(jnp.int32, (SLOTS, GATE_LANES), 1)

        @pl.loop(0, groups)
        def _(g):
            gates = gates_ref[pl.ds(pl.multiple_of(g * GROUP, GROUP), GROUP), :]
            st = slots_of_group(ids, gates, before)
            st_ref[g] = st[:, : 2 * SLOTS].astype(jnp.bfloat16)
            pick = jnp.transpose(st)[: 2 * SLOTS].astype(jnp.bfloat16)
            pick_ref[g] = pick
            picked = jnp.dot(pick, gates, preferred_element_type=jnp.float32)
            for e in range(2):
                own = picked[e * SLOTS : (e + 1) * SLOTS]
                wanted = (slot_lane == ids[e]) | (slot_lane == ids[e] + EXPERTS)
                own = jnp.sum(jnp.where(wanted, own, 0.0), axis=1, keepdims=True)
                gate_ref[e, pl.ds(pl.multiple_of(g * SLOTS, 16), SLOTS), :] = jnp.broadcast_to(
                    own, (SLOTS, GATE_LANES)
                )

    @pl.loop(0, groups)
    def _(g):
        x = x_ref[pl.ds(pl.multiple_of(g * GROUP, GROUP), GROUP), :]
        rows = jnp.dot(pick_ref[g], x, preferred_element_type=jnp.float32).astype(jnp.bfloat16)
        for e in range(2):
            rows_ref[e, pl.ds(pl.multiple_of(g * SLOTS, 16), SLOTS), :] = rows[
                e * SLOTS : (e + 1) * SLOTS
            ]

    for e, pair in enumerate(((wg0, wu0), (wg1, wu1))):
        for which, w in enumerate(pair):

            @pl.loop(0, rows_ref.shape[1] // chunk)
            def _(m):
                part = pl.ds(pl.multiple_of(m * chunk, 16), chunk)
                acc_ref[e, which, part, :] += jnp.dot(
                    rows_ref[e, part, :], w[...], preferred_element_type=jnp.float32
                )

    @pl.when(step == steps - 1)
    def _():
        for e in range(2):

            @pl.loop(0, rows_ref.shape[1] // chunk)
            def _(m):
                part = pl.ds(pl.multiple_of(m * chunk, 16), chunk)
                gate_part = acc_ref[e, 0, part, :]
                hidden = gate_part / (1.0 + jnp.exp(-gate_part)) * acc_ref[e, 1, part, :]
                hid_ref[e, part, :] = (hidden * gate_ref[e, part, 0:1]).astype(jnp.bfloat16)


def hidden_call(ids, gathered, up_weights, width, ff):
    tokens = gathered.shape[0]
    tile = min(512, width)
    groups = tokens // GROUP
    rows = groups * SLOTS
    weight = pl.BlockSpec((tile, ff), lambda n, ids: (n, 0))
    return pl.pallas_call(
        hidden_kernel,
        out_shape=(
            jax.ShapeDtypeStruct((2, rows, ff), jnp.bfloat16),
            jax.ShapeDtypeStruct((groups, GROUP, 2 * SLOTS), jnp.bfloat16),
        ),
        grid_spec=pltpu.PrefetchScalarGridSpec(
            num_scalar_prefetch=1,
            grid=(width // tile,),
            in_specs=[
                pl.BlockSpec((tokens, GATE_LANES), lambda n, ids: (0, width // GATE_LANES)),
                pl.BlockSpec((tokens, tile), lambda n, ids: (0, n)),
                weight, weight, weight, weight,
            ],
            out_specs=(
                pl.BlockSpec((2, rows, ff), lambda n, ids: (0, 0, 0)),
                pl.BlockSpec((groups, GROUP, 2 * SLOTS), lambda n, ids: (0, 0, 0)),
            ),
            scratch_shapes=[
                pltpu.VMEM((groups, 2 * SLOTS, GROUP), jnp.bfloat16),
                pltpu.VMEM((2, rows, GATE_LANES), jnp.float32),
                pltpu.VMEM((2, rows, tile), jnp.bfloat16),
                pltpu.VMEM((2, 2, rows, ff), jnp.float32),
            ],
        ),
        compiler_params=pltpu.CompilerParams(
            dimension_semantics=("arbitrary",), vmem_limit_bytes=52 << 20
        ),
        cost_estimate=pl.CostEstimate(
            flops=8 * rows * width * ff, bytes_accessed=2 * tokens * width, transcendentals=0
        ),
        name="hidden",
    )(ids, gathered, gathered, *up_weights)


def down_kernel(plane_first, plane, hid_ref, st_ref, wd0, wd1, o_ref, y_ref):
    groups = st_ref.shape[0]
    batch = groups // 4
    chunk = batch * SLOTS
    for e, w in enumerate((wd0, wd1)):

        @pl.loop(0, 4)
        def _(m):
            part = jnp.dot(
                hid_ref[e, pl.ds(pl.multiple_of(m * chunk, 16), chunk), :],
                w[...],
                preferred_element_type=jnp.float32,
            ).astype(jnp.bfloat16)
            for j in range(batch):
                y_ref[m * batch + j, e * SLOTS : (e + 1) * SLOTS, :] = part[
                    j * SLOTS : (j + 1) * SLOTS
                ]

    half = pl.program_id(0)

    @pl.loop(0, groups)
    def _(g):
        out = jnp.dot(st_ref[g], y_ref[g], preferred_element_type=jnp.float32)
        out = out.astype(jnp.bfloat16)
        z, y = g // RING, g % RING
        if plane_first:
            ahead, behind = (plane[0] + 3 - z) & 3, (z + 3 - plane[0]) & 3
            stop = jnp.where(half == 0, ahead, behind)
            o_ref[0, stop, pl.ds(pl.multiple_of(y * GROUP, GROUP), GROUP), :] = out
        else:
            for b in range(RING):
                o_ref[y * RING + b, z, :, :] = out[b * TOK : (b + 1) * TOK]


def down_call(plane, hidden, chosen, down_weights, first, tile, count, plane_first):
    rows, ff = hidden.shape[1:]
    groups = chosen.shape[0]
    columns = tile * count
    skip = first // tile
    whole = lambda shape: pl.BlockSpec(
        shape, lambda n, plane: (0, 0, 0), pipeline_mode=pl.Buffered(1)
    )
    weight = pl.BlockSpec((ff, tile), lambda n, plane: (0, n + skip))
    if plane_first:
        shape = (count, RING, RING * GROUP, tile)
        block = pl.BlockSpec((1,) + shape[1:], lambda n, plane: (n, 0, 0, 0))
    else:
        shape = (RING * RING, RING, TOK, columns)
        block = pl.BlockSpec(shape[:3] + (tile,), lambda n, plane: (0, 0, 0, n))
    return pl.pallas_call(
        functools.partial(down_kernel, plane_first),
        out_shape=jax.ShapeDtypeStruct(shape, jnp.bfloat16),
        grid_spec=pltpu.PrefetchScalarGridSpec(
            num_scalar_prefetch=1,
            grid=(count,),
            in_specs=[
                whole(hidden.shape), whole(chosen.shape), weight, weight,
            ],
            out_specs=block,
            scratch_shapes=[pltpu.VMEM((groups, 2 * SLOTS, tile), jnp.bfloat16)],
        ),
        compiler_params=pltpu.CompilerParams(
            dimension_semantics=("arbitrary",), vmem_limit_bytes=40 << 20
        ),
        cost_estimate=pl.CostEstimate(
            flops=4 * rows * columns * ff,
            bytes_accessed=2 * groups * GROUP * columns,
            transcendentals=0,
        ),
        name="down_plane" if plane_first else "down",
    )(plane, hidden, chosen, *down_weights)


def add_rounded(a, b):
    return (a.astype(jnp.float32) + b.astype(jnp.float32)).astype(jnp.bfloat16)


def body(
    streams, phi_matrix, mix_scale, mix_bias, router, expert_index_table, w_gate, w_up, down_weight
):
    width, ff = w_gate.shape[1], w_gate.shape[2]
    swap = [(0, 1), (1, 0)]
    own = (w_gate[0], w_up[0], down_weight[0])
    other = tuple(lax.ppermute(w, "c", swap) for w in own)
    pre, post, mixing = mix_coefficients(streams, phi_matrix, mix_scale, mix_bias)
    layer_in = mix_input(streams, pre)
    gates = dense_gates(layer_in, router, expert_index_table)
    packed = jnp.concatenate([layer_in, gates], axis=1)
    gathered = lax.all_gather(packed, ("z", "y", "x"), axis=0, tiled=True)
    core = lax.axis_index("c")
    pair = 2 * (lax.axis_index("y") * RING + lax.axis_index("x"))
    ids = jnp.stack([pair + core, pair + 1 - core]).astype(jnp.int32)
    plane = lax.axis_index("z")
    planes = plane.reshape(1).astype(jnp.int32)
    ups, downs = own[:2] + other[:2], (own[2], other[2])
    hidden, chosen = hidden_call(ids, gathered, ups, width, ff)
    late = width - PLANE_COLS
    dense = down_call(planes, hidden, chosen, downs, PLANE_COLS, 256, late // 256, False)
    summed = lax.psum_scatter(
        dense.reshape(-1, late), ("y", "x"), scatter_dimension=0, tiled=True
    ).reshape(RING, TOK, late)
    halves = down_call(planes, hidden, chosen, downs, 0, PLANE_COLS // 2, 2, True)
    travel = [halves[0, 0], halves[1, 0]]
    for stop in range(1, RING):
        for way, turn in ((0, 1), (1, RING - 1)):
            ring = [(i, (i + turn) % RING) for i in range(RING)]
            travel[way] = add_rounded(lax.ppermute(travel[way], "z", ring), halves[way, stop])
    early_out = lax.psum_scatter(
        jnp.concatenate(travel, axis=1), ("y", "x"), scatter_dimension=0, tiled=True
    ).astype(jnp.float32)
    late_out = lax.dynamic_index_in_dim(summed, plane, 0, keepdims=False).astype(jnp.float32)
    for shift in range(1, RING):
        away = lax.dynamic_index_in_dim(summed, (plane + shift) % RING, 0, keepdims=False)
        ring = [(i, (i + shift) % RING) for i in range(RING)]
        late_out = late_out + lax.ppermute(away, "z", ring).astype(jnp.float32)
    moe_out = jnp.concatenate([early_out, late_out], axis=1)
    return mix_output(streams, mixing, post, moe_out)


def solution(mesh):
    torus = Mesh(mesh.devices.reshape(RING, RING, RING, 2), ("z", "y", "x", "c"))
    tokens, experts = ("z", "y", "x", "c"), ("y", "x", "c")
    in_specs = (
        P(tokens, None, None),
        P(),
        P(),
        P(),
        P(),
        P(tokens, None),
        P(experts, None, "z"),
        P(experts, None, "z"),
        P(experts, "z", None),
    )
    out_specs = P(tokens, None, None)
    return jax.shard_map(
        body, mesh=torus, in_specs=in_specs, out_specs=out_specs, check_vma=False
    )
```

```python
import functools

import jax
import jax.numpy as jnp
from jax import lax
from jax.experimental import pallas as pl
from jax.experimental.pallas import tpu as pltpu
from jax.sharding import Mesh, PartitionSpec as P

BALANCE_SWEEPS = 20
EXPERTS = 32
CAP = 20
TOK = 64
GROUP = 256
SLOTS = GROUP // TOK * CAP
GATE_LANES = 128
RING = 4
PLANE_COLS = 1280


def balance_kernel(logits_ref, out_ref):
    cells = tuple(jnp.exp(logits_ref[i : i + 1, :]) for i in range(16))

    def sweep(step, cells):
        rows = [cells[4 * n] + cells[4 * n + 1] + cells[4 * n + 2] + cells[4 * n + 3] for n in range(4)]
        cells = [cells[i] / rows[i // 4] for i in range(16)]
        cols = [cells[m] + cells[4 + m] + cells[8 + m] + cells[12 + m] for m in range(4)]
        return tuple(cells[i] / cols[i % 4] for i in range(16))

    cells = lax.fori_loop(0, BALANCE_SWEEPS, sweep, cells)
    for i in range(16):
        out_ref[i : i + 1, :] = cells[i]


def balance_call(logits):
    return pl.pallas_call(
        balance_kernel,
        out_shape=jax.ShapeDtypeStruct(logits.shape, jnp.float32),
        in_specs=[pl.BlockSpec(memory_space=pltpu.VMEM)],
        out_specs=pl.BlockSpec(memory_space=pltpu.VMEM),
        cost_estimate=pl.CostEstimate(flops=100000, bytes_accessed=8192, transcendentals=1024),
        name="balance",
    )(logits)


def mix_coefficients(streams, phi_matrix, mix_scale, mix_bias):
    count = streams.shape[1]
    flat = streams.astype(jnp.float32).reshape(streams.shape[0], -1)
    normed = flat * lax.rsqrt(jnp.mean(flat * flat, axis=1, keepdims=True) + 1e-06)
    normed = normed.astype(jnp.bfloat16)
    coeffs = lax.dot_general(
        normed, phi_matrix, (((1,), (1,)), ((), ())), preferred_element_type=jnp.float32
    )
    pre = jax.nn.sigmoid(mix_scale[0] * coeffs[:, :count] + mix_bias[:count])
    post = 2.0 * jax.nn.sigmoid(
        mix_scale[1] * coeffs[:, count : 2 * count] + mix_bias[count : 2 * count]
    )
    logits = mix_scale[2] * coeffs[:, 2 * count :] + mix_bias[2 * count :]
    mixing = balance_call(logits.T).T.reshape(-1, count, count)
    return (pre, post, mixing)


def mix_input(streams, pre):
    total = pre[:, 0, None] * streams[:, 0, :].astype(jnp.float32)
    for stream in range(1, streams.shape[1]):
        total = total + pre[:, stream, None] * streams[:, stream, :].astype(jnp.float32)
    return total.astype(jnp.bfloat16)


def mix_output(streams, mixing, post, moe_out):
    rows = []
    for target in range(streams.shape[1]):
        total = mixing[:, target, 0, None] * streams[:, 0, :].astype(jnp.float32)
        for source in range(1, streams.shape[1]):
            total = total + mixing[:, target, source, None] * streams[:, source, :].astype(
                jnp.float32
            )
        rows.append(total + post[:, target, None] * moe_out)
    return jnp.stack(rows, axis=1).astype(jnp.bfloat16)


def dense_gates(layer_in, router, expert_index_table):
    logits = lax.dot_general(
        layer_in, router, (((1,), (1,)), ((), ())), preferred_element_type=jnp.float32
    )
    affinity = jax.nn.sigmoid(logits)
    experts = lax.iota(jnp.int32, EXPERTS)
    named = jnp.any(expert_index_table[:, :, None] == experts[None, None, :], axis=1)
    chosen = jnp.where(named, affinity, 0.0)
    gates = 2.5 * chosen / jnp.sum(chosen, axis=1, keepdims=True)
    high = lax.reduce_precision(gates, 8, 7)
    low = gates - high
    pad = jnp.zeros((gates.shape[0], GATE_LANES - 2 * EXPERTS), jnp.float32)
    return jnp.concatenate([high, low, pad], axis=1).astype(jnp.bfloat16)


def slot_tables(ids):
    slot = lax.broadcasted_iota(jnp.int32, (2 * SLOTS, GATE_LANES), 0)
    lane = lax.broadcasted_iota(jnp.int32, (2 * SLOTS, GATE_LANES), 1)
    expert = jnp.where(slot < SLOTS, ids[0], ids[1])
    return lane == expert, lane == expert + EXPERTS


def place_of(slot, token):
    inner = lax.rem(slot, SLOTS)
    return jnp.where(inner // CAP == token // TOK, lax.rem(inner, CAP) + 1, -1)


def pick_kernel(ids, x_ref, rows_ref, gate_ref, st_ref):
    width = rows_ref.shape[-1]
    tile = min(512, width)
    gates = x_ref[:, width : width + GATE_LANES]
    hit = (gates.astype(jnp.float32) != 0.0).astype(jnp.float32)
    row = lax.broadcasted_iota(jnp.int32, (GROUP, GROUP), 0)
    col = lax.broadcasted_iota(jnp.int32, (GROUP, GROUP), 1)
    upto = ((col <= row) & (col // TOK == row // TOK)).astype(jnp.float32).astype(jnp.bfloat16)
    count = jnp.dot(upto, hit.astype(jnp.bfloat16), preferred_element_type=jnp.float32)
    count = (count * hit).astype(jnp.bfloat16)
    high, low = slot_tables(ids)
    table = high.astype(jnp.float32).astype(jnp.bfloat16)
    across = (((1,), (1,)), ((), ()))
    by_slot = lax.dot_general(table, count, across, preferred_element_type=jnp.float32)
    slot = lax.broadcasted_iota(jnp.int32, (2 * SLOTS, GROUP), 0)
    token = lax.broadcasted_iota(jnp.int32, (2 * SLOTS, GROUP), 1)
    pick = by_slot == place_of(slot, token).astype(jnp.float32)
    pick = pick.astype(jnp.float32).astype(jnp.bfloat16)
    by_token = lax.dot_general(count, table, across, preferred_element_type=jnp.float32)
    token = lax.broadcasted_iota(jnp.int32, (GROUP, 2 * SLOTS), 0)
    slot = lax.broadcasted_iota(jnp.int32, (GROUP, 2 * SLOTS), 1)
    put = by_token == place_of(slot, token).astype(jnp.float32)
    st_ref[0] = put.astype(jnp.float32).astype(jnp.bfloat16)
    for n in range(width // tile):
        cols = slice(n * tile, (n + 1) * tile)
        rows = jnp.dot(pick, x_ref[:, cols], preferred_element_type=jnp.float32)
        rows = rows.astype(jnp.bfloat16)
        rows_ref[0, :, cols] = rows[:SLOTS]
        rows_ref[1, :, cols] = rows[SLOTS:]
    picked = jnp.dot(pick, gates, preferred_element_type=jnp.float32)
    own = jnp.sum(jnp.where(high | low, picked, 0.0), axis=1, keepdims=True)
    own = jnp.broadcast_to(own, (2 * SLOTS, GATE_LANES))
    gate_ref[0] = own[:SLOTS]
    gate_ref[1] = own[SLOTS:]


def pick_call(ids, gathered, width):
    groups = gathered.shape[0] // GROUP
    return pl.pallas_call(
        pick_kernel,
        out_shape=(
            jax.ShapeDtypeStruct((2, groups * SLOTS, width), jnp.bfloat16),
            jax.ShapeDtypeStruct((2, groups * SLOTS, GATE_LANES), jnp.float32),
            jax.ShapeDtypeStruct((groups, GROUP, 2 * SLOTS), jnp.bfloat16),
        ),
        grid_spec=pltpu.PrefetchScalarGridSpec(
            num_scalar_prefetch=1,
            grid=(groups,),
            in_specs=[pl.BlockSpec((GROUP, width + GATE_LANES), lambda g, ids: (g, 0))],
            out_specs=(
                pl.BlockSpec((2, SLOTS, width), lambda g, ids: (0, g, 0)),
                pl.BlockSpec((2, SLOTS, GATE_LANES), lambda g, ids: (0, g, 0)),
                pl.BlockSpec((1, GROUP, 2 * SLOTS), lambda g, ids: (g, 0, 0)),
            ),
        ),
        compiler_params=pltpu.CompilerParams(
            dimension_semantics=("arbitrary",), vmem_limit_bytes=24 << 20
        ),
        cost_estimate=pl.CostEstimate(
            flops=4 * groups * SLOTS * GROUP * width,
            bytes_accessed=4 * groups * GROUP * width,
            transcendentals=0,
        ),
        name="pick",
    )(ids, gathered)


def put_kernel(halves, plane, st_ref, y0_ref, y1_ref, *outs):
    columns = y0_ref.shape[-1]
    tile = columns // halves if halves > 1 else min(256, columns)
    for n in range(columns // tile):
        cols = slice(n * tile, (n + 1) * tile)
        y = jnp.concatenate([y0_ref[:, cols], y1_ref[:, cols]], axis=0)
        out = jnp.dot(st_ref[0], y, preferred_element_type=jnp.float32).astype(jnp.bfloat16)
        if halves > 1:
            outs[n][0] = out
        else:
            for b in range(RING):
                outs[0][b, 0, :, cols] = out[b * TOK : (b + 1) * TOK]


def put_call(plane, chosen, y0, y1, halves):
    groups = chosen.shape[0]
    columns = y0.shape[1]
    if halves > 1:
        half = columns // halves
        shape = jax.ShapeDtypeStruct((RING, RING * GROUP, half), jnp.bfloat16)
        out_shape = (shape, shape)
        out_specs = (
            pl.BlockSpec(
                (1, GROUP, half), lambda g, plane: ((plane[0] + 3 - g // RING) & 3, g % RING, 0)
            ),
            pl.BlockSpec(
                (1, GROUP, half), lambda g, plane: ((g // RING + 3 - plane[0]) & 3, g % RING, 0)
            ),
        )
    else:
        out_shape = jax.ShapeDtypeStruct((RING * RING, RING, TOK, columns), jnp.bfloat16)
        out_specs = pl.BlockSpec(
            (RING, 1, TOK, columns), lambda g, plane: (g % RING, g // RING, 0, 0)
        )
    return pl.pallas_call(
        functools.partial(put_kernel, halves),
        out_shape=out_shape,
        grid_spec=pltpu.PrefetchScalarGridSpec(
            num_scalar_prefetch=1,
            grid=(groups,),
            in_specs=[
                pl.BlockSpec((1, GROUP, 2 * SLOTS), lambda g, plane: (g, 0, 0)),
                pl.BlockSpec((SLOTS, columns), lambda g, plane: (g, 0)),
                pl.BlockSpec((SLOTS, columns), lambda g, plane: (g, 0)),
            ],
            out_specs=out_specs,
        ),
        compiler_params=pltpu.CompilerParams(
            dimension_semantics=("arbitrary",), vmem_limit_bytes=24 << 20
        ),
        cost_estimate=pl.CostEstimate(
            flops=4 * groups * GROUP * SLOTS * columns,
            bytes_accessed=3 * groups * GROUP * columns,
            transcendentals=0,
        ),
        name="put_halves" if halves > 1 else "put",
    )(plane, chosen, y0, y1)


def run_hidden(rows, gate, w_gate, w_up):
    gate_part = jnp.dot(rows, w_gate, preferred_element_type=jnp.float32)
    up_part = jnp.dot(rows, w_up, preferred_element_type=jnp.float32)
    return (jax.nn.silu(gate_part) * up_part * gate[:, :1]).astype(jnp.bfloat16)


def run_down(hidden, down_weight):
    return jnp.dot(hidden, down_weight, preferred_element_type=jnp.float32).astype(jnp.bfloat16)


def add_rounded(a, b):
    return (a.astype(jnp.float32) + b.astype(jnp.float32)).astype(jnp.bfloat16)


def body(
    streams, phi_matrix, mix_scale, mix_bias, router, expert_index_table, w_gate, w_up, down_weight
):
    width, ff = w_gate.shape[1], w_gate.shape[2]
    swap = [(0, 1), (1, 0)]
    own = (w_gate[0], w_up[0], down_weight[0])
    other = tuple(lax.ppermute(w, "c", swap) for w in own)
    pre, post, mixing = mix_coefficients(streams, phi_matrix, mix_scale, mix_bias)
    layer_in = mix_input(streams, pre)
    gates = dense_gates(layer_in, router, expert_index_table)
    packed = jnp.concatenate([layer_in, gates], axis=1)
    gathered = lax.all_gather(packed, ("z", "y", "x"), axis=0, tiled=True)
    core = lax.axis_index("c")
    pair = 2 * (lax.axis_index("y") * RING + lax.axis_index("x"))
    ids = jnp.stack([pair + core, pair + 1 - core]).astype(jnp.int32)
    plane = lax.axis_index("z")
    planes = plane.reshape(1).astype(jnp.int32)
    rows, gate, chosen = pick_call(ids, gathered, width)
    hidden = [run_hidden(rows[e], gate[e], *w[:2]) for e, w in enumerate((own, other))]
    hidden = lax.optimization_barrier(hidden)
    downs = (own[2], other[2])
    late = width - PLANE_COLS
    late_parts = [run_down(h, w[:, :late]) for h, w in zip(hidden, downs)]
    dense = put_call(planes, chosen, *late_parts, 1)
    summed = lax.psum_scatter(
        dense.reshape(-1, late), ("y", "x"), scatter_dimension=0, tiled=True
    ).reshape(RING, TOK, late)
    early_parts = [run_down(h, w[:, late:]) for h, w in zip(hidden, downs)]
    halves = put_call(planes, chosen, *early_parts, 2)
    travel = [half[0] for half in halves]
    for stop in range(1, RING):
        for way, turn in ((0, 1), (1, RING - 1)):
            ring = [(i, (i + turn) % RING) for i in range(RING)]
            travel[way] = add_rounded(lax.ppermute(travel[way], "z", ring), halves[way][stop])
    shares = jnp.concatenate(travel, axis=1).reshape(RING * RING, TOK, PLANE_COLS)
    shares = lax.all_to_all(shares, ("y", "x"), split_axis=0, concat_axis=0, tiled=True)
    early_out = jnp.sum(shares.astype(jnp.float32), axis=0)
    late_out = lax.dynamic_index_in_dim(summed, plane, 0, keepdims=False).astype(jnp.float32)
    for shift in range(1, RING):
        away = lax.dynamic_index_in_dim(summed, (plane + shift) % RING, 0, keepdims=False)
        ring = [(i, (i + shift) % RING) for i in range(RING)]
        late_out = late_out + lax.ppermute(away, "z", ring).astype(jnp.float32)
    moe_out = jnp.concatenate([late_out, early_out], axis=1)
    return mix_output(streams, mixing, post, moe_out)


def solution(mesh):
    torus = Mesh(mesh.devices.reshape(RING, RING, RING, 2), ("z", "y", "x", "c"))
    tokens, experts = ("z", "y", "x", "c"), ("y", "x", "c")
    in_specs = (
        P(tokens, None, None),
        P(),
        P(),
        P(),
        P(),
        P(tokens, None),
        P(experts, None, "z"),
        P(experts, None, "z"),
        P(experts, "z", None),
    )
    out_specs = P(tokens, None, None)
    return jax.shard_map(
        body, mesh=torus, in_specs=in_specs, out_specs=out_specs, check_vma=False
    )
```

```python
import functools

import jax
import jax.numpy as jnp
from jax import lax
from jax.experimental import pallas as pl
from jax.experimental.pallas import tpu as pltpu
from jax.sharding import Mesh, PartitionSpec as P

BALANCE_SWEEPS = 20
EXPERTS = 32
CAP = 20
TOK = 64
GROUP = 256
SLOTS = GROUP // TOK * CAP
GATE_LANES = 128
RING = 4
PLANE_COLS = 1280


def balance_kernel(logits_ref, out_ref):
    cells = tuple(jnp.exp(logits_ref[i : i + 1, :]) for i in range(16))

    def sweep(step, cells):
        rows = [cells[4 * n] + cells[4 * n + 1] + cells[4 * n + 2] + cells[4 * n + 3] for n in range(4)]
        cells = [cells[i] / rows[i // 4] for i in range(16)]
        cols = [cells[m] + cells[4 + m] + cells[8 + m] + cells[12 + m] for m in range(4)]
        return tuple(cells[i] / cols[i % 4] for i in range(16))

    cells = lax.fori_loop(0, BALANCE_SWEEPS, sweep, cells)
    for i in range(16):
        out_ref[i : i + 1, :] = cells[i]


def balance_call(logits):
    return pl.pallas_call(
        balance_kernel,
        out_shape=jax.ShapeDtypeStruct(logits.shape, jnp.float32),
        in_specs=[pl.BlockSpec(memory_space=pltpu.VMEM)],
        out_specs=pl.BlockSpec(memory_space=pltpu.VMEM),
        cost_estimate=pl.CostEstimate(flops=100000, bytes_accessed=8192, transcendentals=1024),
        name="balance",
    )(logits)


def mix_coefficients(streams, phi_matrix, mix_scale, mix_bias):
    count = streams.shape[1]
    flat = streams.astype(jnp.float32).reshape(streams.shape[0], -1)
    normed = flat * lax.rsqrt(jnp.mean(flat * flat, axis=1, keepdims=True) + 1e-06)
    normed = normed.astype(jnp.bfloat16)
    coeffs = lax.dot_general(
        normed, phi_matrix, (((1,), (1,)), ((), ())), preferred_element_type=jnp.float32
    )
    pre = jax.nn.sigmoid(mix_scale[0] * coeffs[:, :count] + mix_bias[:count])
    post = 2.0 * jax.nn.sigmoid(
        mix_scale[1] * coeffs[:, count : 2 * count] + mix_bias[count : 2 * count]
    )
    logits = mix_scale[2] * coeffs[:, 2 * count :] + mix_bias[2 * count :]
    mixing = balance_call(logits.T).T.reshape(-1, count, count)
    return (pre, post, mixing)


def mix_input(streams, pre):
    total = pre[:, 0, None] * streams[:, 0, :].astype(jnp.float32)
    for stream in range(1, streams.shape[1]):
        total = total + pre[:, stream, None] * streams[:, stream, :].astype(jnp.float32)
    return total.astype(jnp.bfloat16)


def mix_output(streams, mixing, post, moe_out):
    rows = []
    for target in range(streams.shape[1]):
        total = mixing[:, target, 0, None] * streams[:, 0, :].astype(jnp.float32)
        for source in range(1, streams.shape[1]):
            total = total + mixing[:, target, source, None] * streams[:, source, :].astype(
                jnp.float32
            )
        rows.append(total + post[:, target, None] * moe_out)
    return jnp.stack(rows, axis=1).astype(jnp.bfloat16)


def dense_gates(layer_in, router, expert_index_table):
    logits = lax.dot_general(
        layer_in, router, (((1,), (1,)), ((), ())), preferred_element_type=jnp.float32
    )
    affinity = jax.nn.sigmoid(logits)
    experts = lax.iota(jnp.int32, EXPERTS)
    named = jnp.any(expert_index_table[:, :, None] == experts[None, None, :], axis=1)
    chosen = jnp.where(named, affinity, 0.0)
    gates = 2.5 * chosen / jnp.sum(chosen, axis=1, keepdims=True)
    high = lax.reduce_precision(gates, 8, 7)
    low = gates - high
    pad = jnp.zeros((gates.shape[0], GATE_LANES - 2 * EXPERTS), jnp.float32)
    return jnp.concatenate([high, low, pad], axis=1).astype(jnp.bfloat16)


def slot_tables(ids):
    slot = lax.broadcasted_iota(jnp.int32, (2 * SLOTS, GATE_LANES), 0)
    lane = lax.broadcasted_iota(jnp.int32, (2 * SLOTS, GATE_LANES), 1)
    expert = jnp.where(slot < SLOTS, ids[0], ids[1])
    return lane == expert, lane == expert + EXPERTS


def place_of(slot, token):
    inner = lax.rem(slot, SLOTS)
    return jnp.where(inner // CAP == token // TOK, lax.rem(inner, CAP) + 1, -1)


def pick_kernel(ids, x_ref, rows_ref, gate_ref, st_ref, upto_ref, want_ref, wanted_ref):
    width = rows_ref.shape[-1]
    tile = min(512, width)
    across = (((1,), (1,)), ((), ()))

    @pl.when(pl.program_id(0) == 0)
    def _():
        row = lax.broadcasted_iota(jnp.int32, (GROUP, GROUP), 0)
        col = lax.broadcasted_iota(jnp.int32, (GROUP, GROUP), 1)
        upto = (col <= row) & (col // TOK == row // TOK)
        upto_ref[...] = upto.astype(jnp.float32).astype(jnp.bfloat16)
        slot = lax.broadcasted_iota(jnp.int32, (2 * SLOTS, GROUP), 0)
        token = lax.broadcasted_iota(jnp.int32, (2 * SLOTS, GROUP), 1)
        want_ref[...] = place_of(slot, token).astype(jnp.float32)
        token = lax.broadcasted_iota(jnp.int32, (GROUP, 2 * SLOTS), 0)
        slot = lax.broadcasted_iota(jnp.int32, (GROUP, 2 * SLOTS), 1)
        wanted_ref[...] = place_of(slot, token).astype(jnp.float32)

    high, low = slot_tables(ids)
    table = high.astype(jnp.float32).astype(jnp.bfloat16)
    for g in range(x_ref.shape[0] // GROUP):
        tokens = slice(g * GROUP, (g + 1) * GROUP)
        mine = slice(g * SLOTS, (g + 1) * SLOTS)
        gates = x_ref[tokens, width : width + GATE_LANES]
        hit = (gates.astype(jnp.float32) != 0.0).astype(jnp.float32)
        count = jnp.dot(
            upto_ref[...], hit.astype(jnp.bfloat16), preferred_element_type=jnp.float32
        )
        count = (count * hit).astype(jnp.bfloat16)
        by_slot = lax.dot_general(table, count, across, preferred_element_type=jnp.float32)
        pick = (by_slot == want_ref[...]).astype(jnp.float32).astype(jnp.bfloat16)
        by_token = lax.dot_general(count, table, across, preferred_element_type=jnp.float32)
        put = (by_token == wanted_ref[...]).astype(jnp.float32)
        st_ref[g] = put.astype(jnp.bfloat16)
        for n in range(width // tile):
            cols = slice(n * tile, (n + 1) * tile)
            rows = jnp.dot(pick, x_ref[tokens, cols], preferred_element_type=jnp.float32)
            rows = rows.astype(jnp.bfloat16)
            rows_ref[0, mine, cols] = rows[:SLOTS]
            rows_ref[1, mine, cols] = rows[SLOTS:]
        picked = jnp.dot(pick, gates, preferred_element_type=jnp.float32)
        picked = jnp.where(high | low, picked, 0.0)
        gate_ref[0, mine] = picked[:SLOTS]
        gate_ref[1, mine] = picked[SLOTS:]


def pick_call(ids, gathered, width):
    groups = gathered.shape[0] // GROUP
    step = 2
    return pl.pallas_call(
        pick_kernel,
        out_shape=(
            jax.ShapeDtypeStruct((2, groups * SLOTS, width), jnp.bfloat16),
            jax.ShapeDtypeStruct((2, groups * SLOTS, GATE_LANES), jnp.float32),
            jax.ShapeDtypeStruct((groups, GROUP, 2 * SLOTS), jnp.bfloat16),
        ),
        grid_spec=pltpu.PrefetchScalarGridSpec(
            num_scalar_prefetch=1,
            grid=(groups // step,),
            in_specs=[pl.BlockSpec((step * GROUP, width + GATE_LANES), lambda g, ids: (g, 0))],
            out_specs=(
                pl.BlockSpec((2, step * SLOTS, width), lambda g, ids: (0, g, 0)),
                pl.BlockSpec((2, step * SLOTS, GATE_LANES), lambda g, ids: (0, g, 0)),
                pl.BlockSpec((step, GROUP, 2 * SLOTS), lambda g, ids: (g, 0, 0)),
            ),
            scratch_shapes=[
                pltpu.VMEM((GROUP, GROUP), jnp.bfloat16),
                pltpu.VMEM((2 * SLOTS, GROUP), jnp.float32),
                pltpu.VMEM((GROUP, 2 * SLOTS), jnp.float32),
            ],
        ),
        compiler_params=pltpu.CompilerParams(
            dimension_semantics=("arbitrary",), vmem_limit_bytes=26 << 20
        ),
        cost_estimate=pl.CostEstimate(
            flops=4 * groups * SLOTS * GROUP * width,
            bytes_accessed=4 * groups * GROUP * width,
            transcendentals=0,
        ),
        name="pick",
    )(ids, gathered)


def put_kernel(halves, plane, st_ref, y_ref, *outs):
    columns = y_ref.shape[-1]
    tile = columns // halves if halves > 1 else min(256, columns)

    @pl.loop(0, RING)
    def _(g):
        mine = pl.ds(pl.multiple_of(g * SLOTS, 16), SLOTS)
        for n in range(columns // tile):
            cols = slice(n * tile, (n + 1) * tile)
            y = jnp.concatenate([y_ref[0, mine, cols], y_ref[1, mine, cols]], axis=0)
            out = jnp.dot(st_ref[g], y, preferred_element_type=jnp.float32)
            out = out.astype(jnp.bfloat16)
            if halves > 1:
                outs[n][0, pl.ds(pl.multiple_of(g * GROUP, GROUP), GROUP), :] = out
            else:
                for b in range(RING):
                    outs[0][g * RING + b, 0, :, cols] = out[b * TOK : (b + 1) * TOK]


def put_call(plane, chosen, y, halves):
    groups = chosen.shape[0]
    columns = y.shape[-1]
    if halves > 1:
        half = columns // halves
        shape = jax.ShapeDtypeStruct((RING, RING * GROUP, half), jnp.bfloat16)
        out_shape = (shape, shape)
        block = (1, RING * GROUP, half)
        out_specs = (
            pl.BlockSpec(block, lambda z, plane: ((plane[0] + 3 - z) & 3, 0, 0)),
            pl.BlockSpec(block, lambda z, plane: ((z + 3 - plane[0]) & 3, 0, 0)),
        )
    else:
        out_shape = jax.ShapeDtypeStruct((RING * RING, RING, TOK, columns), jnp.bfloat16)
        out_specs = pl.BlockSpec(
            (RING * RING, 1, TOK, columns), lambda z, plane: (0, z, 0, 0)
        )
    return pl.pallas_call(
        functools.partial(put_kernel, halves),
        out_shape=out_shape,
        grid_spec=pltpu.PrefetchScalarGridSpec(
            num_scalar_prefetch=1,
            grid=(groups // RING,),
            in_specs=[
                pl.BlockSpec((RING, GROUP, 2 * SLOTS), lambda z, plane: (z, 0, 0)),
                pl.BlockSpec((2, RING * SLOTS, columns), lambda z, plane: (0, z, 0)),
            ],
            out_specs=out_specs,
        ),
        compiler_params=pltpu.CompilerParams(
            dimension_semantics=("arbitrary",), vmem_limit_bytes=26 << 20
        ),
        cost_estimate=pl.CostEstimate(
            flops=4 * groups * GROUP * SLOTS * columns,
            bytes_accessed=3 * groups * GROUP * columns,
            transcendentals=0,
        ),
        name="put_halves" if halves > 1 else "put",
    )(plane, chosen, y)


def run_hidden(rows, gate, w_gate, w_up):
    gate = jnp.sum(gate, axis=2, keepdims=True)
    gate_part = jnp.einsum("erd,edf->erf", rows, w_gate, preferred_element_type=jnp.float32)
    up_part = jnp.einsum("erd,edf->erf", rows, w_up, preferred_element_type=jnp.float32)
    return (jax.nn.silu(gate_part) * up_part * gate).astype(jnp.bfloat16)


def run_down(hidden, down_weight):
    part = jnp.einsum("erf,efd->erd", hidden, down_weight, preferred_element_type=jnp.float32)
    return part.astype(jnp.bfloat16)


def add_rounded(a, b):
    return (a.astype(jnp.float32) + b.astype(jnp.float32)).astype(jnp.bfloat16)


def body(
    streams, phi_matrix, mix_scale, mix_bias, router, expert_index_table, w_gate, w_up, down_weight
):
    width, ff = w_gate.shape[1], w_gate.shape[2]
    swap = [(0, 1), (1, 0)]
    own = (w_gate[0], w_up[0], down_weight[0])
    other = tuple(lax.ppermute(w, "c", swap) for w in own)
    pre, post, mixing = mix_coefficients(streams, phi_matrix, mix_scale, mix_bias)
    layer_in = mix_input(streams, pre)
    gates = dense_gates(layer_in, router, expert_index_table)
    packed = jnp.concatenate([layer_in, gates], axis=1)
    gathered = lax.all_gather(packed, ("z", "y", "x"), axis=0, tiled=True)
    core = lax.axis_index("c")
    pair = 2 * (lax.axis_index("y") * RING + lax.axis_index("x"))
    ids = jnp.stack([pair + core, pair + 1 - core]).astype(jnp.int32)
    plane = lax.axis_index("z")
    planes = plane.reshape(1).astype(jnp.int32)
    rows, gate, chosen = pick_call(ids, gathered, width)
    late = width - PLANE_COLS
    w_gates, w_ups = (jnp.stack(pair) for pair in zip(own[:2], other[:2]))
    late_downs = jnp.stack([own[2][:, :late], other[2][:, :late]])
    early_downs = jnp.stack([own[2][:, late:], other[2][:, late:]])
    hidden = lax.optimization_barrier(run_hidden(rows, gate, w_gates, w_ups))
    dense = put_call(planes, chosen, run_down(hidden, late_downs), 1)
    summed = lax.psum_scatter(
        dense.reshape(-1, late), ("y", "x"), scatter_dimension=0, tiled=True
    ).reshape(RING, TOK, late)
    halves = put_call(planes, chosen, run_down(hidden, early_downs), 2)
    travel = [half[0] for half in halves]
    for stop in range(1, RING):
        for way, turn in ((0, 1), (1, RING - 1)):
            ring = [(i, (i + turn) % RING) for i in range(RING)]
            travel[way] = add_rounded(lax.ppermute(travel[way], "z", ring), halves[way][stop])
    shares = jnp.concatenate(travel, axis=1).reshape(RING * RING, TOK, PLANE_COLS)
    shares = lax.all_to_all(shares, ("y", "x"), split_axis=0, concat_axis=0, tiled=True)
    early_out = jnp.sum(shares.astype(jnp.float32), axis=0)
    late_out = lax.dynamic_index_in_dim(summed, plane, 0, keepdims=False).astype(jnp.float32)
    for shift in range(1, RING):
        away = lax.dynamic_index_in_dim(summed, (plane + shift) % RING, 0, keepdims=False)
        ring = [(i, (i + shift) % RING) for i in range(RING)]
        late_out = late_out + lax.ppermute(away, "z", ring).astype(jnp.float32)
    moe_out = jnp.concatenate([late_out, early_out], axis=1)
    return mix_output(streams, mixing, post, moe_out)


def solution(mesh):
    torus = Mesh(mesh.devices.reshape(RING, RING, RING, 2), ("z", "y", "x", "c"))
    tokens, experts = ("z", "y", "x", "c"), ("y", "x", "c")
    in_specs = (
        P(tokens, None, None),
        P(),
        P(),
        P(),
        P(),
        P(tokens, None),
        P(experts, None, "z"),
        P(experts, None, "z"),
        P(experts, "z", None),
    )
    out_specs = P(tokens, None, None)
    return jax.shard_map(
        body, mesh=torus, in_specs=in_specs, out_specs=out_specs, check_vma=False
    )
```

```python
import functools

import jax
import jax.numpy as jnp
from jax import lax
from jax.experimental import pallas as pl
from jax.experimental.pallas import tpu as pltpu
from jax.sharding import Mesh, PartitionSpec as P

BALANCE_SWEEPS = 20
EXPERTS = 32
CAP = 20
TOK = 64
GROUP = 256
SLOTS = GROUP // TOK * CAP
GATE_LANES = 128
RING = 4
PLANE_COLS = 1536
CHUNKS = 2


def balance_kernel(logits_ref, out_ref):
    cells = tuple(jnp.exp(logits_ref[i : i + 1, :]) for i in range(16))

    def sweep(step, cells):
        rows = [cells[4 * n] + cells[4 * n + 1] + cells[4 * n + 2] + cells[4 * n + 3] for n in range(4)]
        cells = [cells[i] / rows[i // 4] for i in range(16)]
        cols = [cells[m] + cells[4 + m] + cells[8 + m] + cells[12 + m] for m in range(4)]
        return tuple(cells[i] / cols[i % 4] for i in range(16))

    cells = lax.fori_loop(0, BALANCE_SWEEPS, sweep, cells)
    for i in range(16):
        out_ref[i : i + 1, :] = cells[i]


def balance_call(logits):
    return pl.pallas_call(
        balance_kernel,
        out_shape=jax.ShapeDtypeStruct(logits.shape, jnp.float32),
        in_specs=[pl.BlockSpec(memory_space=pltpu.VMEM)],
        out_specs=pl.BlockSpec(memory_space=pltpu.VMEM),
        cost_estimate=pl.CostEstimate(flops=100000, bytes_accessed=8192, transcendentals=1024),
        name="balance",
    )(logits)


def mix_coefficients(streams, phi_matrix, mix_scale, mix_bias):
    count = streams.shape[1]
    flat = streams.astype(jnp.float32).reshape(streams.shape[0], -1)
    normed = flat * lax.rsqrt(jnp.mean(flat * flat, axis=1, keepdims=True) + 1e-06)
    normed = normed.astype(jnp.bfloat16)
    coeffs = lax.dot_general(
        normed, phi_matrix, (((1,), (1,)), ((), ())), preferred_element_type=jnp.float32
    )
    pre = jax.nn.sigmoid(mix_scale[0] * coeffs[:, :count] + mix_bias[:count])
    post = 2.0 * jax.nn.sigmoid(
        mix_scale[1] * coeffs[:, count : 2 * count] + mix_bias[count : 2 * count]
    )
    logits = mix_scale[2] * coeffs[:, 2 * count :] + mix_bias[2 * count :]
    mixing = balance_call(logits.T).T.reshape(-1, count, count)
    return (pre, post, mixing)


def mix_input(streams, pre):
    total = pre[:, 0, None] * streams[:, 0, :].astype(jnp.float32)
    for stream in range(1, streams.shape[1]):
        total = total + pre[:, stream, None] * streams[:, stream, :].astype(jnp.float32)
    return total.astype(jnp.bfloat16)


def mix_output(streams, mixing, post, moe_out):
    rows = []
    for target in range(streams.shape[1]):
        total = mixing[:, target, 0, None] * streams[:, 0, :].astype(jnp.float32)
        for source in range(1, streams.shape[1]):
            total = total + mixing[:, target, source, None] * streams[:, source, :].astype(
                jnp.float32
            )
        rows.append(total + post[:, target, None] * moe_out)
    return jnp.stack(rows, axis=1).astype(jnp.bfloat16)


def dense_gates(layer_in, router, expert_index_table):
    logits = lax.dot_general(
        layer_in, router, (((1,), (1,)), ((), ())), preferred_element_type=jnp.float32
    )
    affinity = jax.nn.sigmoid(logits)
    experts = lax.iota(jnp.int32, EXPERTS)
    named = jnp.any(expert_index_table[:, :, None] == experts[None, None, :], axis=1)
    chosen = jnp.where(named, affinity, 0.0)
    gates = 2.5 * chosen / jnp.sum(chosen, axis=1, keepdims=True)
    high = lax.reduce_precision(gates, 8, 7)
    low = gates - high
    pad = jnp.zeros((gates.shape[0], GATE_LANES - 2 * EXPERTS), jnp.float32)
    return jnp.concatenate([high, low, pad], axis=1).astype(jnp.bfloat16)


def slot_tables(ids):
    slot = lax.broadcasted_iota(jnp.int32, (2 * SLOTS, GATE_LANES), 0)
    lane = lax.broadcasted_iota(jnp.int32, (2 * SLOTS, GATE_LANES), 1)
    expert = jnp.where(slot < SLOTS, ids[0], ids[1])
    return lane == expert, lane == expert + EXPERTS


def place_of(slot, token):
    inner = lax.rem(slot, SLOTS)
    return jnp.where(inner // CAP == token // TOK, lax.rem(inner, CAP) + 1, -1)


def pick_kernel(ids, x_ref, rows_ref, gate_ref, st_ref, upto_ref, want_ref, wanted_ref):
    width = rows_ref.shape[-1]
    tile = min(512, width)
    across = (((1,), (1,)), ((), ()))

    @pl.when(pl.program_id(0) == 0)
    def _():
        row = lax.broadcasted_iota(jnp.int32, (GROUP, GROUP), 0)
        col = lax.broadcasted_iota(jnp.int32, (GROUP, GROUP), 1)
        upto = (col <= row) & (col // TOK == row // TOK)
        upto_ref[...] = upto.astype(jnp.float32).astype(jnp.bfloat16)
        slot = lax.broadcasted_iota(jnp.int32, (2 * SLOTS, GROUP), 0)
        token = lax.broadcasted_iota(jnp.int32, (2 * SLOTS, GROUP), 1)
        want_ref[...] = place_of(slot, token).astype(jnp.float32)
        token = lax.broadcasted_iota(jnp.int32, (GROUP, 2 * SLOTS), 0)
        slot = lax.broadcasted_iota(jnp.int32, (GROUP, 2 * SLOTS), 1)
        wanted_ref[...] = place_of(slot, token).astype(jnp.float32)

    high, low = slot_tables(ids)
    table = high.astype(jnp.float32).astype(jnp.bfloat16)

    @pl.loop(0, x_ref.shape[0] // GROUP)
    def _(g):
        tokens = pl.ds(pl.multiple_of(g * GROUP, GROUP), GROUP)
        mine = pl.ds(pl.multiple_of(g * SLOTS, 16), SLOTS)
        gates = x_ref[tokens, width : width + GATE_LANES]
        hit = (gates.astype(jnp.float32) != 0.0).astype(jnp.float32)
        count = jnp.dot(
            upto_ref[...], hit.astype(jnp.bfloat16), preferred_element_type=jnp.float32
        )
        count = (count * hit).astype(jnp.bfloat16)
        by_slot = lax.dot_general(table, count, across, preferred_element_type=jnp.float32)
        pick = (by_slot == want_ref[...]).astype(jnp.float32).astype(jnp.bfloat16)
        by_token = lax.dot_general(count, table, across, preferred_element_type=jnp.float32)
        put = (by_token == wanted_ref[...]).astype(jnp.float32)
        st_ref[g] = put.astype(jnp.bfloat16)
        for n in range(width // tile):
            cols = slice(n * tile, (n + 1) * tile)
            rows = jnp.dot(pick, x_ref[tokens, cols], preferred_element_type=jnp.float32)
            rows = rows.astype(jnp.bfloat16)
            rows_ref[0, mine, cols] = rows[:SLOTS]
            rows_ref[1, mine, cols] = rows[SLOTS:]
        picked = jnp.dot(pick, gates, preferred_element_type=jnp.float32)
        picked = jnp.where(high | low, picked, 0.0)
        gate_ref[0, mine] = picked[:SLOTS]
        gate_ref[1, mine] = picked[SLOTS:]


def pick_call(ids, gathered, width):
    groups = gathered.shape[0] // GROUP
    step = 2
    return pl.pallas_call(
        pick_kernel,
        out_shape=(
            jax.ShapeDtypeStruct((2, groups * SLOTS, width), jnp.bfloat16),
            jax.ShapeDtypeStruct((2, groups * SLOTS, GATE_LANES), jnp.float32),
            jax.ShapeDtypeStruct((groups, GROUP, 2 * SLOTS), jnp.bfloat16),
        ),
        grid_spec=pltpu.PrefetchScalarGridSpec(
            num_scalar_prefetch=1,
            grid=(groups // step,),
            in_specs=[pl.BlockSpec((step * GROUP, width + GATE_LANES), lambda g, ids: (g, 0))],
            out_specs=(
                pl.BlockSpec((2, step * SLOTS, width), lambda g, ids: (0, g, 0)),
                pl.BlockSpec((2, step * SLOTS, GATE_LANES), lambda g, ids: (0, g, 0)),
                pl.BlockSpec((step, GROUP, 2 * SLOTS), lambda g, ids: (g, 0, 0)),
            ),
            scratch_shapes=[
                pltpu.VMEM((GROUP, GROUP), jnp.bfloat16),
                pltpu.VMEM((2 * SLOTS, GROUP), jnp.float32),
                pltpu.VMEM((GROUP, 2 * SLOTS), jnp.float32),
            ],
        ),
        compiler_params=pltpu.CompilerParams(
            dimension_semantics=("arbitrary",), vmem_limit_bytes=50 << 20
        ),
        cost_estimate=pl.CostEstimate(
            flops=4 * groups * SLOTS * GROUP * width,
            bytes_accessed=4 * groups * GROUP * width,
            transcendentals=0,
        ),
        name="pick",
    )(ids, gathered)


def put_kernel(halves, plane, st_ref, y_ref, *outs):
    columns = y_ref.shape[-1]
    tile = columns // halves if halves > 1 else min(256, columns)

    @pl.loop(0, RING)
    def _(g):
        mine = pl.ds(pl.multiple_of(g * SLOTS, 16), SLOTS)
        for n in range(columns // tile):
            cols = slice(n * tile, (n + 1) * tile)
            y = jnp.concatenate([y_ref[0, mine, cols], y_ref[1, mine, cols]], axis=0)
            out = jnp.dot(st_ref[g], y, preferred_element_type=jnp.float32)
            out = out.astype(jnp.bfloat16)
            if halves > 1:
                outs[n][0, pl.ds(pl.multiple_of(g * GROUP, GROUP), GROUP), :] = out
            else:
                for b in range(RING):
                    outs[0][g * RING + b, 0, :, cols] = out[b * TOK : (b + 1) * TOK]


def put_call(plane, chosen, y, halves):
    groups = chosen.shape[0]
    columns = y.shape[-1]
    if halves > 1:
        half = columns // halves
        shape = jax.ShapeDtypeStruct((RING, RING * GROUP, half), jnp.bfloat16)
        out_shape = (shape,) * halves
        block = (1, RING * GROUP, half)
        out_specs = (
            pl.BlockSpec(block, lambda z, plane: ((plane[0] + 3 - z) & 3, 0, 0)),
            pl.BlockSpec(block, lambda z, plane: ((z + 3 - plane[0]) & 3, 0, 0)),
        ) * (halves // 2)
    else:
        out_shape = jax.ShapeDtypeStruct((RING * RING, RING, TOK, columns), jnp.bfloat16)
        out_specs = pl.BlockSpec(
            (RING * RING, 1, TOK, columns), lambda z, plane: (0, z, 0, 0)
        )
    return pl.pallas_call(
        functools.partial(put_kernel, halves),
        out_shape=out_shape,
        grid_spec=pltpu.PrefetchScalarGridSpec(
            num_scalar_prefetch=1,
            grid=(groups // RING,),
            in_specs=[
                pl.BlockSpec((RING, GROUP, 2 * SLOTS), lambda z, plane: (z, 0, 0)),
                pl.BlockSpec((2, RING * SLOTS, columns), lambda z, plane: (0, z, 0)),
            ],
            out_specs=out_specs,
        ),
        compiler_params=pltpu.CompilerParams(
            dimension_semantics=("arbitrary",), vmem_limit_bytes=26 << 20
        ),
        cost_estimate=pl.CostEstimate(
            flops=4 * groups * GROUP * SLOTS * columns,
            bytes_accessed=3 * groups * GROUP * columns,
            transcendentals=0,
        ),
        name="put_halves" if halves > 1 else "put",
    )(plane, chosen, y)


def run_hidden(rows, gate, w_gate, w_up):
    gate = jnp.sum(gate, axis=2, keepdims=True)
    gate_part = jnp.einsum("erd,edf->erf", rows, w_gate, preferred_element_type=jnp.float32)
    up_part = jnp.einsum("erd,edf->erf", rows, w_up, preferred_element_type=jnp.float32)
    return (jax.nn.silu(gate_part) * up_part * gate).astype(jnp.bfloat16)


def run_down(hidden, down_weight):
    part = jnp.einsum("erf,efd->erd", hidden, down_weight, preferred_element_type=jnp.float32)
    return part.astype(jnp.bfloat16)


def add_rounded(a, b):
    return (a.astype(jnp.float32) + b.astype(jnp.float32)).astype(jnp.bfloat16)


def body(
    streams, phi_matrix, mix_scale, mix_bias, router, expert_index_table, w_gate, w_up, down_weight
):
    width, ff = w_gate.shape[1], w_gate.shape[2]
    swap = [(0, 1), (1, 0)]
    own = (w_gate[0], w_up[0], down_weight[0])
    other = tuple(lax.ppermute(w, "c", swap) for w in own)
    pre, post, mixing = mix_coefficients(streams, phi_matrix, mix_scale, mix_bias)
    layer_in = mix_input(streams, pre)
    gates = dense_gates(layer_in, router, expert_index_table)
    packed = jnp.concatenate([layer_in, gates], axis=1)
    gathered = lax.all_gather(packed, ("z", "y", "x"), axis=0, tiled=True)
    core = lax.axis_index("c")
    pair = 2 * (lax.axis_index("y") * RING + lax.axis_index("x"))
    ids = jnp.stack([pair + core, pair + 1 - core]).astype(jnp.int32)
    plane = lax.axis_index("z")
    planes = plane.reshape(1).astype(jnp.int32)
    late = width - PLANE_COLS
    w_gates, w_ups = (jnp.stack(pair) for pair in zip(own[:2], other[:2]))
    late_downs = jnp.stack([own[2][:, :late], other[2][:, :late]])
    early_downs = jnp.stack([own[2][:, late:], other[2][:, late:]])
    gathered, late_downs, early_downs = lax.optimization_barrier(
        (gathered, late_downs, early_downs)
    )
    rows, gate, chosen = pick_call(ids, gathered, width)
    hidden = lax.optimization_barrier(run_hidden(rows, gate, w_gates, w_ups))
    dense = put_call(planes, chosen, run_down(hidden, late_downs), 1)
    summed = lax.psum_scatter(
        dense.reshape(-1, late), ("y", "x"), scatter_dimension=0, tiled=True
    ).reshape(RING, TOK, late)
    halves = put_call(planes, chosen, run_down(hidden, early_downs), 2 * CHUNKS)
    travel = [half[0] for half in halves]
    for stop in range(1, RING):
        for part in range(2 * CHUNKS):
            turn = (1, RING - 1)[part % 2]
            ring = [(i, (i + turn) % RING) for i in range(RING)]
            travel[part] = add_rounded(lax.ppermute(travel[part], "z", ring), halves[part][stop])
    early_out = []
    for chunk in range(CHUNKS):
        shares = jnp.concatenate(travel[2 * chunk : 2 * chunk + 2], axis=1)
        shares = shares.reshape(RING * RING, TOK, PLANE_COLS // CHUNKS)
        shares = lax.all_to_all(shares, ("y", "x"), split_axis=0, concat_axis=0, tiled=True)
        early_out.append(jnp.sum(shares.astype(jnp.float32), axis=0))
    late_out = lax.dynamic_index_in_dim(summed, plane, 0, keepdims=False).astype(jnp.float32)
    for shift in range(1, RING):
        away = lax.dynamic_index_in_dim(summed, (plane + shift) % RING, 0, keepdims=False)
        ring = [(i, (i + shift) % RING) for i in range(RING)]
        late_out = late_out + lax.ppermute(away, "z", ring).astype(jnp.float32)
    moe_out = jnp.concatenate([late_out] + early_out, axis=1)
    return mix_output(streams, mixing, post, moe_out)


def solution(mesh):
    torus = Mesh(mesh.devices.reshape(RING, RING, RING, 2), ("z", "y", "x", "c"))
    tokens, experts = ("z", "y", "x", "c"), ("y", "x", "c")
    in_specs = (
        P(tokens, None, None),
        P(),
        P(),
        P(),
        P(),
        P(tokens, None),
        P(experts, None, "z"),
        P(experts, None, "z"),
        P(experts, "z", None),
    )
    out_specs = P(tokens, None, None)
    return jax.shard_map(
        body, mesh=torus, in_specs=in_specs, out_specs=out_specs, check_vma=False
    )
```

```python
import functools

import jax
import jax.numpy as jnp
from jax import lax
from jax.experimental import pallas as pl
from jax.experimental.pallas import tpu as pltpu
from jax.sharding import Mesh, PartitionSpec as P

BALANCE_SWEEPS = 20
EXPERTS = 32
CAP = 20
TOK = 64
GROUP = 256
SLOTS = GROUP // TOK * CAP
GATE_LANES = 128
RING = 4
CHUNKS = (512, 768)


def balance_kernel(logits_ref, out_ref):
    cells = tuple(jnp.exp(logits_ref[i : i + 1, :]) for i in range(16))

    def sweep(step, cells):
        rows = [cells[4 * n] + cells[4 * n + 1] + cells[4 * n + 2] + cells[4 * n + 3] for n in range(4)]
        cells = [cells[i] / rows[i // 4] for i in range(16)]
        cols = [cells[m] + cells[4 + m] + cells[8 + m] + cells[12 + m] for m in range(4)]
        return tuple(cells[i] / cols[i % 4] for i in range(16))

    cells = lax.fori_loop(0, BALANCE_SWEEPS, sweep, cells)
    for i in range(16):
        out_ref[i : i + 1, :] = cells[i]


def balance_call(logits):
    return pl.pallas_call(
        balance_kernel,
        out_shape=jax.ShapeDtypeStruct(logits.shape, jnp.float32),
        in_specs=[pl.BlockSpec(memory_space=pltpu.VMEM)],
        out_specs=pl.BlockSpec(memory_space=pltpu.VMEM),
        cost_estimate=pl.CostEstimate(flops=100000, bytes_accessed=8192, transcendentals=1024),
        name="balance",
    )(logits)


def mix_coefficients(streams, phi_matrix, mix_scale, mix_bias):
    count = streams.shape[1]
    flat = streams.astype(jnp.float32).reshape(streams.shape[0], -1)
    normed = flat * lax.rsqrt(jnp.mean(flat * flat, axis=1, keepdims=True) + 1e-06)
    normed = normed.astype(jnp.bfloat16)
    coeffs = lax.dot_general(
        normed, phi_matrix, (((1,), (1,)), ((), ())), preferred_element_type=jnp.float32
    )
    pre = jax.nn.sigmoid(mix_scale[0] * coeffs[:, :count] + mix_bias[:count])
    post = 2.0 * jax.nn.sigmoid(
        mix_scale[1] * coeffs[:, count : 2 * count] + mix_bias[count : 2 * count]
    )
    logits = mix_scale[2] * coeffs[:, 2 * count :] + mix_bias[2 * count :]
    mixing = balance_call(logits.T).T.reshape(-1, count, count)
    return (pre, post, mixing)


def mix_input(streams, pre):
    total = pre[:, 0, None] * streams[:, 0, :].astype(jnp.float32)
    for stream in range(1, streams.shape[1]):
        total = total + pre[:, stream, None] * streams[:, stream, :].astype(jnp.float32)
    return total.astype(jnp.bfloat16)


def mix_output(streams, mixing, post, moe_out):
    rows = []
    for target in range(streams.shape[1]):
        total = mixing[:, target, 0, None] * streams[:, 0, :].astype(jnp.float32)
        for source in range(1, streams.shape[1]):
            total = total + mixing[:, target, source, None] * streams[:, source, :].astype(
                jnp.float32
            )
        rows.append(total + post[:, target, None] * moe_out)
    return jnp.stack(rows, axis=1).astype(jnp.bfloat16)


def dense_gates(layer_in, router, expert_index_table):
    logits = lax.dot_general(
        layer_in, router, (((1,), (1,)), ((), ())), preferred_element_type=jnp.float32
    )
    affinity = jax.nn.sigmoid(logits)
    experts = lax.iota(jnp.int32, EXPERTS)
    named = jnp.any(expert_index_table[:, :, None] == experts[None, None, :], axis=1)
    chosen = jnp.where(named, affinity, 0.0)
    gates = 2.5 * chosen / jnp.sum(chosen, axis=1, keepdims=True)
    high = lax.reduce_precision(gates, 8, 7)
    low = gates - high
    pad = jnp.zeros((gates.shape[0], GATE_LANES - 2 * EXPERTS), jnp.float32)
    return jnp.concatenate([high, low, pad], axis=1).astype(jnp.bfloat16)


def slot_tables(ids):
    slot = lax.broadcasted_iota(jnp.int32, (2 * SLOTS, GATE_LANES), 0)
    lane = lax.broadcasted_iota(jnp.int32, (2 * SLOTS, GATE_LANES), 1)
    expert = jnp.where(slot < SLOTS, ids[0], ids[1])
    return lane == expert, lane == expert + EXPERTS


def place_of(slot, token):
    inner = lax.rem(slot, SLOTS)
    return jnp.where(inner // CAP == token // TOK, lax.rem(inner, CAP) + 1, -1)


def pick_kernel(ids, x_ref, rows_ref, gate_ref, st_ref, upto_ref, want_ref, wanted_ref):
    width = rows_ref.shape[-1]
    tile = min(512, width)
    across = (((1,), (1,)), ((), ()))

    @pl.when(pl.program_id(0) == 0)
    def _():
        row = lax.broadcasted_iota(jnp.int32, (GROUP, GROUP), 0)
        col = lax.broadcasted_iota(jnp.int32, (GROUP, GROUP), 1)
        upto = (col <= row) & (col // TOK == row // TOK)
        upto_ref[...] = upto.astype(jnp.float32).astype(jnp.bfloat16)
        slot = lax.broadcasted_iota(jnp.int32, (2 * SLOTS, GROUP), 0)
        token = lax.broadcasted_iota(jnp.int32, (2 * SLOTS, GROUP), 1)
        want_ref[...] = place_of(slot, token).astype(jnp.float32)
        token = lax.broadcasted_iota(jnp.int32, (GROUP, 2 * SLOTS), 0)
        slot = lax.broadcasted_iota(jnp.int32, (GROUP, 2 * SLOTS), 1)
        wanted_ref[...] = place_of(slot, token).astype(jnp.float32)

    high, low = slot_tables(ids)
    table = high.astype(jnp.float32).astype(jnp.bfloat16)

    @pl.loop(0, x_ref.shape[0] // GROUP)
    def _(g):
        tokens = pl.ds(pl.multiple_of(g * GROUP, GROUP), GROUP)
        mine = pl.ds(pl.multiple_of(g * SLOTS, 16), SLOTS)
        gates = x_ref[tokens, width : width + GATE_LANES]
        hit = (gates.astype(jnp.float32) != 0.0).astype(jnp.float32)
        count = jnp.dot(
            upto_ref[...], hit.astype(jnp.bfloat16), preferred_element_type=jnp.float32
        )
        count = (count * hit).astype(jnp.bfloat16)
        by_slot = lax.dot_general(table, count, across, preferred_element_type=jnp.float32)
        pick = (by_slot == want_ref[...]).astype(jnp.float32).astype(jnp.bfloat16)
        by_token = lax.dot_general(count, table, across, preferred_element_type=jnp.float32)
        put = (by_token == wanted_ref[...]).astype(jnp.float32)
        st_ref[g] = put.astype(jnp.bfloat16)
        for n in range(width // tile):
            cols = slice(n * tile, (n + 1) * tile)
            rows = jnp.dot(pick, x_ref[tokens, cols], preferred_element_type=jnp.float32)
            rows = rows.astype(jnp.bfloat16)
            rows_ref[0, mine, cols] = rows[:SLOTS]
            rows_ref[1, mine, cols] = rows[SLOTS:]
        picked = jnp.dot(pick, gates, preferred_element_type=jnp.float32)
        picked = jnp.where(high | low, picked, 0.0)
        gate_ref[0, mine] = picked[:SLOTS]
        gate_ref[1, mine] = picked[SLOTS:]


def pick_call(ids, gathered, width):
    groups = gathered.shape[0] // GROUP
    step = 2
    return pl.pallas_call(
        pick_kernel,
        out_shape=(
            jax.ShapeDtypeStruct((2, groups * SLOTS, width), jnp.bfloat16),
            jax.ShapeDtypeStruct((2, groups * SLOTS, GATE_LANES), jnp.float32),
            jax.ShapeDtypeStruct((groups, GROUP, 2 * SLOTS), jnp.bfloat16),
        ),
        grid_spec=pltpu.PrefetchScalarGridSpec(
            num_scalar_prefetch=1,
            grid=(groups // step,),
            in_specs=[pl.BlockSpec((step * GROUP, width + GATE_LANES), lambda g, ids: (g, 0))],
            out_specs=(
                pl.BlockSpec((2, step * SLOTS, width), lambda g, ids: (0, g, 0)),
                pl.BlockSpec((2, step * SLOTS, GATE_LANES), lambda g, ids: (0, g, 0)),
                pl.BlockSpec((step, GROUP, 2 * SLOTS), lambda g, ids: (g, 0, 0)),
            ),
            scratch_shapes=[
                pltpu.VMEM((GROUP, GROUP), jnp.bfloat16),
                pltpu.VMEM((2 * SLOTS, GROUP), jnp.float32),
                pltpu.VMEM((GROUP, 2 * SLOTS), jnp.float32),
            ],
        ),
        compiler_params=pltpu.CompilerParams(
            dimension_semantics=("arbitrary",), vmem_limit_bytes=26 << 20
        ),
        cost_estimate=pl.CostEstimate(
            flops=4 * groups * SLOTS * GROUP * width,
            bytes_accessed=4 * groups * GROUP * width,
            transcendentals=0,
        ),
        name="pick",
    )(ids, gathered)


def put_kernel(widths, plane, st_ref, y0_ref, y1_ref, *outs):
    columns = y0_ref.shape[-1]
    tile = min(256, columns)
    cuts = widths or (tile,) * (columns // tile)

    @pl.loop(0, RING)
    def _(g):
        mine = pl.ds(pl.multiple_of(g * SLOTS, 16), SLOTS)
        for n, cut in enumerate(cuts):
            cols = slice(sum(cuts[:n]), sum(cuts[: n + 1]))
            y = jnp.concatenate([y0_ref[mine, cols], y1_ref[mine, cols]], axis=0)
            out = jnp.dot(st_ref[g], y, preferred_element_type=jnp.float32)
            out = out.astype(jnp.bfloat16)
            if widths:
                outs[n][0, pl.ds(pl.multiple_of(g * GROUP, GROUP), GROUP), :] = out
            else:
                for b in range(RING):
                    outs[0][g * RING + b, 0, :, cols] = out[b * TOK : (b + 1) * TOK]


def put_call(plane, chosen, y0, y1, widths=()):
    groups = chosen.shape[0]
    columns = y0.shape[-1]
    turns = (lambda z, plane: ((plane[0] + 3 - z) & 3, 0, 0)), (
        lambda z, plane: ((z + 3 - plane[0]) & 3, 0, 0)
    )
    if widths:
        out_shape = tuple(
            jax.ShapeDtypeStruct((RING, RING * GROUP, cut), jnp.bfloat16) for cut in widths
        )
        out_specs = tuple(
            pl.BlockSpec((1, RING * GROUP, cut), turns[n % 2]) for n, cut in enumerate(widths)
        )
    else:
        out_shape = jax.ShapeDtypeStruct((RING * RING, RING, TOK, columns), jnp.bfloat16)
        out_specs = pl.BlockSpec(
            (RING * RING, 1, TOK, columns), lambda z, plane: (0, z, 0, 0)
        )
    rows = pl.BlockSpec((RING * SLOTS, columns), lambda z, plane: (z, 0))
    return pl.pallas_call(
        functools.partial(put_kernel, widths),
        out_shape=out_shape,
        grid_spec=pltpu.PrefetchScalarGridSpec(
            num_scalar_prefetch=1,
            grid=(groups // RING,),
            in_specs=[
                pl.BlockSpec((RING, GROUP, 2 * SLOTS), lambda z, plane: (z, 0, 0)), rows, rows,
            ],
            out_specs=out_specs,
        ),
        compiler_params=pltpu.CompilerParams(
            dimension_semantics=("arbitrary",), vmem_limit_bytes=26 << 20
        ),
        cost_estimate=pl.CostEstimate(
            flops=4 * groups * GROUP * SLOTS * columns,
            bytes_accessed=3 * groups * GROUP * columns,
            transcendentals=0,
        ),
        name="put_halves" if widths else "put",
    )(plane, chosen, y0, y1)


def run_hidden(rows, gate, w_gate, w_up):
    gate = jnp.sum(gate, axis=1, keepdims=True)
    gate_part = jnp.dot(rows, w_gate, preferred_element_type=jnp.float32)
    up_part = jnp.dot(rows, w_up, preferred_element_type=jnp.float32)
    return (jax.nn.silu(gate_part) * up_part * gate).astype(jnp.bfloat16)


def run_down(hidden, down_weights):
    return [
        jnp.dot(h, w, preferred_element_type=jnp.float32).astype(jnp.bfloat16)
        for h, w in zip(hidden, down_weights)
    ]


def add_rounded(a, b):
    return (a.astype(jnp.float32) + b.astype(jnp.float32)).astype(jnp.bfloat16)


def body(
    streams, phi_matrix, mix_scale, mix_bias, router, expert_index_table, w_gate, w_up, down_weight
):
    width, ff = w_gate.shape[1], w_gate.shape[2]
    swap = [(0, 1), (1, 0)]
    own = (w_gate[0], w_up[0], down_weight[0])
    other = tuple(lax.ppermute(w, "c", swap) for w in own)
    pre, post, mixing = mix_coefficients(streams, phi_matrix, mix_scale, mix_bias)
    layer_in = mix_input(streams, pre)
    gates = dense_gates(layer_in, router, expert_index_table)
    packed = jnp.concatenate([layer_in, gates], axis=1)
    gathered = lax.all_gather(packed, ("z", "y", "x"), axis=0, tiled=True)
    core = lax.axis_index("c")
    pair = 2 * (lax.axis_index("y") * RING + lax.axis_index("x"))
    ids = jnp.stack([pair + core, pair + 1 - core]).astype(jnp.int32)
    plane = lax.axis_index("z")
    planes = plane.reshape(1).astype(jnp.int32)
    late = width - sum(CHUNKS)
    downs = (own[2], other[2])
    late_downs, early_downs = [w[:, :late] for w in downs], [w[:, late:] for w in downs]
    gathered, late_downs, early_downs = lax.optimization_barrier(
        (gathered, late_downs, early_downs)
    )
    rows, gate, chosen = pick_call(ids, gathered, width)
    hidden = [run_hidden(rows[e], gate[e], *w[:2]) for e, w in enumerate((own, other))]
    hidden = lax.optimization_barrier(hidden)
    dense = put_call(planes, chosen, *run_down(hidden, late_downs))
    summed = lax.psum_scatter(
        dense.reshape(-1, late), ("y", "x"), scatter_dimension=0, tiled=True
    ).reshape(RING, TOK, late)
    widths = tuple(cut // 2 for cut in CHUNKS for way in range(2))
    halves = put_call(planes, chosen, *run_down(hidden, early_downs), widths)
    travel = [half[0] for half in halves]
    for stop in range(1, RING):
        for part in range(len(widths)):
            turn = (1, RING - 1)[part % 2]
            ring = [(i, (i + turn) % RING) for i in range(RING)]
            travel[part] = add_rounded(lax.ppermute(travel[part], "z", ring), halves[part][stop])
    early_out = []
    for chunk, cut in enumerate(CHUNKS):
        shares = jnp.concatenate(travel[2 * chunk : 2 * chunk + 2], axis=1)
        shares = shares.reshape(RING * RING, TOK, cut)
        shares = lax.all_to_all(shares, ("y", "x"), split_axis=0, concat_axis=0, tiled=True)
        early_out.append(jnp.sum(shares.astype(jnp.float32), axis=0))
    late_out = lax.dynamic_index_in_dim(summed, plane, 0, keepdims=False).astype(jnp.float32)
    for shift in range(1, RING):
        away = lax.dynamic_index_in_dim(summed, (plane + shift) % RING, 0, keepdims=False)
        ring = [(i, (i + shift) % RING) for i in range(RING)]
        late_out = late_out + lax.ppermute(away, "z", ring).astype(jnp.float32)
    moe_out = jnp.concatenate([late_out] + early_out, axis=1)
    return mix_output(streams, mixing, post, moe_out)


def solution(mesh):
    torus = Mesh(mesh.devices.reshape(RING, RING, RING, 2), ("z", "y", "x", "c"))
    tokens, experts = ("z", "y", "x", "c"), ("y", "x", "c")
    in_specs = (
        P(tokens, None, None),
        P(),
        P(),
        P(),
        P(),
        P(tokens, None),
        P(experts, None, "z"),
        P(experts, None, "z"),
        P(experts, "z", None),
    )
    out_specs = P(tokens, None, None)
    return jax.shard_map(
        body, mesh=torus, in_specs=in_specs, out_specs=out_specs, check_vma=False
    )
```

```python
import functools

import jax
import jax.numpy as jnp
from jax import lax
from jax.experimental import pallas as pl
from jax.experimental.pallas import tpu as pltpu
from jax.sharding import Mesh, PartitionSpec as P

BALANCE_SWEEPS = 20
EXPERTS = 32
CAP = 20
TOK = 64
GROUP = 256
SLOTS = GROUP // TOK * CAP
GATE_LANES = 128
RING = 4
CHUNKS = (512, 768)


def balance_kernel(logits_ref, out_ref):
    cells = tuple(jnp.exp(logits_ref[i : i + 1, :]) for i in range(16))

    def sweep(step, cells):
        rows = [cells[4 * n] + cells[4 * n + 1] + cells[4 * n + 2] + cells[4 * n + 3] for n in range(4)]
        cells = [cells[i] / rows[i // 4] for i in range(16)]
        cols = [cells[m] + cells[4 + m] + cells[8 + m] + cells[12 + m] for m in range(4)]
        return tuple(cells[i] / cols[i % 4] for i in range(16))

    cells = lax.fori_loop(0, BALANCE_SWEEPS, sweep, cells)
    for i in range(16):
        out_ref[i : i + 1, :] = cells[i]


def balance_call(logits):
    return pl.pallas_call(
        balance_kernel,
        out_shape=jax.ShapeDtypeStruct(logits.shape, jnp.float32),
        in_specs=[pl.BlockSpec(memory_space=pltpu.VMEM)],
        out_specs=pl.BlockSpec(memory_space=pltpu.VMEM),
        cost_estimate=pl.CostEstimate(flops=100000, bytes_accessed=8192, transcendentals=1024),
        name="balance",
    )(logits)


def mix_coefficients(streams, phi_matrix, mix_scale, mix_bias):
    count = streams.shape[1]
    flat = streams.astype(jnp.float32).reshape(streams.shape[0], -1)
    normed = flat * lax.rsqrt(jnp.mean(flat * flat, axis=1, keepdims=True) + 1e-06)
    normed = normed.astype(jnp.bfloat16)
    coeffs = lax.dot_general(
        normed, phi_matrix, (((1,), (1,)), ((), ())), preferred_element_type=jnp.float32
    )
    pre = jax.nn.sigmoid(mix_scale[0] * coeffs[:, :count] + mix_bias[:count])
    post = 2.0 * jax.nn.sigmoid(
        mix_scale[1] * coeffs[:, count : 2 * count] + mix_bias[count : 2 * count]
    )
    logits = mix_scale[2] * coeffs[:, 2 * count :] + mix_bias[2 * count :]
    mixing = balance_call(logits.T).T.reshape(-1, count, count)
    return (pre, post, mixing)


def mix_input(streams, pre):
    total = pre[:, 0, None] * streams[:, 0, :].astype(jnp.float32)
    for stream in range(1, streams.shape[1]):
        total = total + pre[:, stream, None] * streams[:, stream, :].astype(jnp.float32)
    return total.astype(jnp.bfloat16)


def mix_output(streams, mixing, post, moe_out):
    rows = []
    for target in range(streams.shape[1]):
        total = mixing[:, target, 0, None] * streams[:, 0, :].astype(jnp.float32)
        for source in range(1, streams.shape[1]):
            total = total + mixing[:, target, source, None] * streams[:, source, :].astype(
                jnp.float32
            )
        rows.append(total + post[:, target, None] * moe_out)
    return jnp.stack(rows, axis=1).astype(jnp.bfloat16)


def dense_gates(layer_in, router, expert_index_table):
    logits = lax.dot_general(
        layer_in, router, (((1,), (1,)), ((), ())), preferred_element_type=jnp.float32
    )
    affinity = jax.nn.sigmoid(logits)
    experts = lax.iota(jnp.int32, EXPERTS)
    named = jnp.any(expert_index_table[:, :, None] == experts[None, None, :], axis=1)
    chosen = jnp.where(named, affinity, 0.0)
    gates = 2.5 * chosen / jnp.sum(chosen, axis=1, keepdims=True)
    high = lax.reduce_precision(gates, 8, 7)
    low = gates - high
    pad = jnp.zeros((gates.shape[0], GATE_LANES - 2 * EXPERTS), jnp.float32)
    return jnp.concatenate([high, low, pad], axis=1).astype(jnp.bfloat16)


def slot_tables(ids):
    slot = lax.broadcasted_iota(jnp.int32, (2 * SLOTS, GATE_LANES), 0)
    lane = lax.broadcasted_iota(jnp.int32, (2 * SLOTS, GATE_LANES), 1)
    expert = jnp.where(slot < SLOTS, ids[0], ids[1])
    return lane == expert, lane == expert + EXPERTS


def place_of(slot, token):
    inner = lax.rem(slot, SLOTS)
    return jnp.where(inner // CAP == token // TOK, lax.rem(inner, CAP) + 1, -1)


def pick_kernel(ids, x0_ref, x1_ref, rows_ref, gate_ref, st_ref, upto_ref, want_ref, wanted_ref):
    width = rows_ref.shape[-1]
    tile = min(512, width)
    across = (((1,), (1,)), ((), ()))

    @pl.when(pl.program_id(0) == 0)
    def _():
        row = lax.broadcasted_iota(jnp.int32, (GROUP, GROUP), 0)
        col = lax.broadcasted_iota(jnp.int32, (GROUP, GROUP), 1)
        upto = (col <= row) & (col // TOK == row // TOK)
        upto_ref[...] = upto.astype(jnp.float32).astype(jnp.bfloat16)
        slot = lax.broadcasted_iota(jnp.int32, (2 * SLOTS, GROUP), 0)
        token = lax.broadcasted_iota(jnp.int32, (2 * SLOTS, GROUP), 1)
        want_ref[...] = place_of(slot, token).astype(jnp.float32)
        token = lax.broadcasted_iota(jnp.int32, (GROUP, 2 * SLOTS), 0)
        slot = lax.broadcasted_iota(jnp.int32, (GROUP, 2 * SLOTS), 1)
        wanted_ref[...] = place_of(slot, token).astype(jnp.float32)

    high, low = slot_tables(ids)
    table = high.astype(jnp.float32).astype(jnp.bfloat16)
    for g, x_ref in enumerate((x0_ref, x1_ref)):
        mine = slice(g * SLOTS, (g + 1) * SLOTS)
        gates = x_ref[:, width : width + GATE_LANES]
        hit = (gates.astype(jnp.float32) != 0.0).astype(jnp.float32)
        count = jnp.dot(
            upto_ref[...], hit.astype(jnp.bfloat16), preferred_element_type=jnp.float32
        )
        count = (count * hit).astype(jnp.bfloat16)
        by_slot = lax.dot_general(table, count, across, preferred_element_type=jnp.float32)
        pick = (by_slot == want_ref[...]).astype(jnp.float32).astype(jnp.bfloat16)
        by_token = lax.dot_general(count, table, across, preferred_element_type=jnp.float32)
        put = (by_token == wanted_ref[...]).astype(jnp.float32)
        st_ref[g] = put.astype(jnp.bfloat16)
        for n in range(width // tile):
            cols = slice(n * tile, (n + 1) * tile)
            rows = jnp.dot(pick, x_ref[:, cols], preferred_element_type=jnp.float32)
            rows = rows.astype(jnp.bfloat16)
            rows_ref[0, mine, cols] = rows[:SLOTS]
            rows_ref[1, mine, cols] = rows[SLOTS:]
        picked = jnp.dot(pick, gates, preferred_element_type=jnp.float32)
        picked = jnp.where(high | low, picked, 0.0)
        gate_ref[0, mine] = picked[:SLOTS]
        gate_ref[1, mine] = picked[SLOTS:]


def pick_call(ids, gathered, width):
    groups = gathered.shape[0] // GROUP
    step = 2
    return pl.pallas_call(
        pick_kernel,
        out_shape=(
            jax.ShapeDtypeStruct((2, groups * SLOTS, width), jnp.bfloat16),
            jax.ShapeDtypeStruct((2, groups * SLOTS, GATE_LANES), jnp.float32),
            jax.ShapeDtypeStruct((groups, GROUP, 2 * SLOTS), jnp.bfloat16),
        ),
        grid_spec=pltpu.PrefetchScalarGridSpec(
            num_scalar_prefetch=1,
            grid=(groups // step,),
            in_specs=[
                pl.BlockSpec((GROUP, width + GATE_LANES), lambda g, ids: (2 * g, 0)),
                pl.BlockSpec((GROUP, width + GATE_LANES), lambda g, ids: (2 * g + 1, 0)),
            ],
            out_specs=(
                pl.BlockSpec((2, step * SLOTS, width), lambda g, ids: (0, g, 0)),
                pl.BlockSpec((2, step * SLOTS, GATE_LANES), lambda g, ids: (0, g, 0)),
                pl.BlockSpec((step, GROUP, 2 * SLOTS), lambda g, ids: (g, 0, 0)),
            ),
            scratch_shapes=[
                pltpu.VMEM((GROUP, GROUP), jnp.bfloat16),
                pltpu.VMEM((2 * SLOTS, GROUP), jnp.float32),
                pltpu.VMEM((GROUP, 2 * SLOTS), jnp.float32),
            ],
        ),
        compiler_params=pltpu.CompilerParams(
            dimension_semantics=("arbitrary",), vmem_limit_bytes=26 << 20
        ),
        cost_estimate=pl.CostEstimate(
            flops=4 * groups * SLOTS * GROUP * width,
            bytes_accessed=4 * groups * GROUP * width,
            transcendentals=0,
        ),
        name="pick",
    )(ids, gathered, gathered)


def put_kernel(widths, plane, st_ref, y0_ref, y1_ref, *outs):
    columns = y0_ref.shape[-1]
    tile = min(256, columns)
    cuts = widths or (tile,) * (columns // tile)

    @pl.loop(0, RING)
    def _(g):
        mine = pl.ds(pl.multiple_of(g * SLOTS, 16), SLOTS)
        for n, cut in enumerate(cuts):
            cols = slice(sum(cuts[:n]), sum(cuts[: n + 1]))
            y = jnp.concatenate([y0_ref[mine, cols], y1_ref[mine, cols]], axis=0)
            out = jnp.dot(st_ref[g], y, preferred_element_type=jnp.float32)
            out = out.astype(jnp.bfloat16)
            if widths:
                outs[n][0, pl.ds(pl.multiple_of(g * GROUP, GROUP), GROUP), :] = out
            else:
                for b in range(RING):
                    outs[0][g * RING + b, 0, :, cols] = out[b * TOK : (b + 1) * TOK]


def put_call(plane, chosen, y0, y1, widths=()):
    groups = chosen.shape[0]
    columns = y0.shape[-1]
    turns = (lambda z, plane: ((plane[0] + 3 - z) & 3, 0, 0)), (
        lambda z, plane: ((z + 3 - plane[0]) & 3, 0, 0)
    )
    if widths:
        out_shape = tuple(
            jax.ShapeDtypeStruct((RING, RING * GROUP, cut), jnp.bfloat16) for cut in widths
        )
        out_specs = tuple(
            pl.BlockSpec((1, RING * GROUP, cut), turns[n % 2]) for n, cut in enumerate(widths)
        )
    else:
        out_shape = jax.ShapeDtypeStruct((RING * RING, RING, TOK, columns), jnp.bfloat16)
        out_specs = pl.BlockSpec(
            (RING * RING, 1, TOK, columns), lambda z, plane: (0, (z + RING - plane[0]) & 3, 0, 0)
        )
    rows = pl.BlockSpec((RING * SLOTS, columns), lambda z, plane: (z, 0))
    return pl.pallas_call(
        functools.partial(put_kernel, widths),
        out_shape=out_shape,
        grid_spec=pltpu.PrefetchScalarGridSpec(
            num_scalar_prefetch=1,
            grid=(groups // RING,),
            in_specs=[
                pl.BlockSpec((RING, GROUP, 2 * SLOTS), lambda z, plane: (z, 0, 0)), rows, rows,
            ],
            out_specs=out_specs,
        ),
        compiler_params=pltpu.CompilerParams(
            dimension_semantics=("arbitrary",), vmem_limit_bytes=26 << 20
        ),
        cost_estimate=pl.CostEstimate(
            flops=4 * groups * GROUP * SLOTS * columns,
            bytes_accessed=3 * groups * GROUP * columns,
            transcendentals=0,
        ),
        name="put_halves" if widths else "put",
    )(plane, chosen, y0, y1)


def run_hidden(rows, gate, w_gate, w_up):
    gate = jnp.sum(gate, axis=1, keepdims=True)
    gate_part = jnp.dot(rows, w_gate, preferred_element_type=jnp.float32)
    up_part = jnp.dot(rows, w_up, preferred_element_type=jnp.float32)
    return (jax.nn.silu(gate_part) * up_part * gate).astype(jnp.bfloat16)


def run_down(hidden, down_weights):
    return [
        jnp.dot(h, w, preferred_element_type=jnp.float32).astype(jnp.bfloat16)
        for h, w in zip(hidden, down_weights)
    ]


def add_rounded(a, b):
    return (a.astype(jnp.float32) + b.astype(jnp.float32)).astype(jnp.bfloat16)


def body(
    streams, phi_matrix, mix_scale, mix_bias, router, expert_index_table, w_gate, w_up, down_weight
):
    width, ff = w_gate.shape[1], w_gate.shape[2]
    swap = [(0, 1), (1, 0)]
    own = (w_gate[0], w_up[0], down_weight[0])
    other = tuple(lax.ppermute(w, "c", swap) for w in own)
    pre, post, mixing = mix_coefficients(streams, phi_matrix, mix_scale, mix_bias)
    layer_in = mix_input(streams, pre)
    gates = dense_gates(layer_in, router, expert_index_table)
    packed = jnp.concatenate([layer_in, gates], axis=1)
    gathered = lax.all_gather(packed, ("z", "y", "x"), axis=0, tiled=True)
    core = lax.axis_index("c")
    pair = 2 * (lax.axis_index("y") * RING + lax.axis_index("x"))
    ids = jnp.stack([pair + core, pair + 1 - core]).astype(jnp.int32)
    plane = lax.axis_index("z")
    planes = plane.reshape(1).astype(jnp.int32)
    late = width - sum(CHUNKS)
    downs = (own[2], other[2])
    late_downs, early_downs = [w[:, :late] for w in downs], [w[:, late:] for w in downs]
    gathered, late_downs, early_downs = lax.optimization_barrier(
        (gathered, late_downs, early_downs)
    )
    rows, gate, chosen = pick_call(ids, gathered, width)
    hidden = [run_hidden(rows[e], gate[e], *w[:2]) for e, w in enumerate((own, other))]
    hidden = lax.optimization_barrier(hidden)
    dense = put_call(planes, chosen, *run_down(hidden, late_downs))
    summed = lax.psum_scatter(
        dense.reshape(-1, late), ("y", "x"), scatter_dimension=0, tiled=True
    ).reshape(RING, TOK, late)
    widths = tuple(cut // 2 for cut in CHUNKS for way in range(2))
    halves = put_call(planes, chosen, *run_down(hidden, early_downs), widths)
    travel = [half[0] for half in halves]
    for stop in range(1, RING):
        for part in range(len(widths)):
            turn = (1, RING - 1)[part % 2]
            ring = [(i, (i + turn) % RING) for i in range(RING)]
            travel[part] = add_rounded(lax.ppermute(travel[part], "z", ring), halves[part][stop])
    early_out = []
    for chunk, cut in enumerate(CHUNKS):
        shares = jnp.concatenate(travel[2 * chunk : 2 * chunk + 2], axis=1)
        shares = shares.reshape(RING * RING, TOK, cut)
        shares = lax.all_to_all(shares, ("y", "x"), split_axis=0, concat_axis=0, tiled=True)
        early_out.append(jnp.sum(shares.astype(jnp.float32), axis=0))
    late_out = summed[0].astype(jnp.float32)
    for shift in range(1, RING):
        ring = [(i, (i + shift) % RING) for i in range(RING)]
        late_out = late_out + lax.ppermute(summed[shift], "z", ring).astype(jnp.float32)
    moe_out = jnp.concatenate([late_out] + early_out, axis=1)
    return mix_output(streams, mixing, post, moe_out)


def solution(mesh):
    torus = Mesh(mesh.devices.reshape(RING, RING, RING, 2), ("z", "y", "x", "c"))
    tokens, experts = ("z", "y", "x", "c"), ("y", "x", "c")
    in_specs = (
        P(tokens, None, None),
        P(),
        P(),
        P(),
        P(),
        P(tokens, None),
        P(experts, None, "z"),
        P(experts, None, "z"),
        P(experts, "z", None),
    )
    out_specs = P(tokens, None, None)
    return jax.shard_map(
        body, mesh=torus, in_specs=in_specs, out_specs=out_specs, check_vma=False
    )
```

```python
import functools

import jax
import jax.numpy as jnp
from jax import lax
from jax.experimental import pallas as pl
from jax.experimental.pallas import tpu as pltpu
from jax.sharding import Mesh, PartitionSpec as P

BALANCE_SWEEPS = 20
EXPERTS = 32
CAP = 20
TOK = 64
GROUP = 256
SLOTS = GROUP // TOK * CAP
GATE_LANES = 128
RING = 4
CHUNKS = (1280,)


def balance_kernel(logits_ref, out_ref):
    cells = tuple(jnp.exp(logits_ref[i : i + 1, :]) for i in range(16))

    def sweep(step, cells):
        rows = [cells[4 * n] + cells[4 * n + 1] + cells[4 * n + 2] + cells[4 * n + 3] for n in range(4)]
        cells = [cells[i] / rows[i // 4] for i in range(16)]
        cols = [cells[m] + cells[4 + m] + cells[8 + m] + cells[12 + m] for m in range(4)]
        return tuple(cells[i] / cols[i % 4] for i in range(16))

    cells = lax.fori_loop(0, BALANCE_SWEEPS, sweep, cells)
    for i in range(16):
        out_ref[i : i + 1, :] = cells[i]


def balance_call(logits):
    return pl.pallas_call(
        balance_kernel,
        out_shape=jax.ShapeDtypeStruct(logits.shape, jnp.float32),
        in_specs=[pl.BlockSpec(memory_space=pltpu.VMEM)],
        out_specs=pl.BlockSpec(memory_space=pltpu.VMEM),
        cost_estimate=pl.CostEstimate(flops=100000, bytes_accessed=8192, transcendentals=1024),
        name="balance",
    )(logits)


def mix_coefficients(streams, phi_matrix, mix_scale, mix_bias):
    count = streams.shape[1]
    flat = streams.astype(jnp.float32).reshape(streams.shape[0], -1)
    normed = flat * lax.rsqrt(jnp.mean(flat * flat, axis=1, keepdims=True) + 1e-06)
    normed = normed.astype(jnp.bfloat16)
    coeffs = lax.dot_general(
        normed, phi_matrix, (((1,), (1,)), ((), ())), preferred_element_type=jnp.float32
    )
    pre = jax.nn.sigmoid(mix_scale[0] * coeffs[:, :count] + mix_bias[:count])
    post = 2.0 * jax.nn.sigmoid(
        mix_scale[1] * coeffs[:, count : 2 * count] + mix_bias[count : 2 * count]
    )
    logits = mix_scale[2] * coeffs[:, 2 * count :] + mix_bias[2 * count :]
    mixing = balance_call(logits.T).T.reshape(-1, count, count)
    return (pre, post, mixing)


def mix_input(streams, pre):
    total = pre[:, 0, None] * streams[:, 0, :].astype(jnp.float32)
    for stream in range(1, streams.shape[1]):
        total = total + pre[:, stream, None] * streams[:, stream, :].astype(jnp.float32)
    return total.astype(jnp.bfloat16)


def mix_output(streams, mixing, post, moe_out):
    rows = []
    for target in range(streams.shape[1]):
        total = mixing[:, target, 0, None] * streams[:, 0, :].astype(jnp.float32)
        for source in range(1, streams.shape[1]):
            total = total + mixing[:, target, source, None] * streams[:, source, :].astype(
                jnp.float32
            )
        rows.append(total + post[:, target, None] * moe_out)
    return jnp.stack(rows, axis=1).astype(jnp.bfloat16)


def dense_gates(layer_in, router, expert_index_table):
    logits = lax.dot_general(
        layer_in, router, (((1,), (1,)), ((), ())), preferred_element_type=jnp.float32
    )
    affinity = jax.nn.sigmoid(logits)
    experts = lax.iota(jnp.int32, EXPERTS)
    named = jnp.any(expert_index_table[:, :, None] == experts[None, None, :], axis=1)
    chosen = jnp.where(named, affinity, 0.0)
    gates = 2.5 * chosen / jnp.sum(chosen, axis=1, keepdims=True)
    high = lax.reduce_precision(gates, 8, 7)
    low = gates - high
    pad = jnp.zeros((gates.shape[0], GATE_LANES - 2 * EXPERTS), jnp.float32)
    return jnp.concatenate([high, low, pad], axis=1).astype(jnp.bfloat16)


def slot_tables(ids):
    slot = lax.broadcasted_iota(jnp.int32, (2 * SLOTS, GATE_LANES), 0)
    lane = lax.broadcasted_iota(jnp.int32, (2 * SLOTS, GATE_LANES), 1)
    expert = jnp.where(slot < SLOTS, ids[0], ids[1])
    return lane == expert, lane == expert + EXPERTS


def place_of(slot, token):
    inner = lax.rem(slot, SLOTS)
    return jnp.where(inner // CAP == token // TOK, lax.rem(inner, CAP) + 1, -1)


def pick_kernel(ids, x_ref, rows_ref, gate_ref, st_ref, upto_ref, want_ref, wanted_ref):
    width = rows_ref.shape[-1]
    tile = min(512, width)
    across = (((1,), (1,)), ((), ()))

    @pl.when(pl.program_id(0) == 0)
    def _():
        row = lax.broadcasted_iota(jnp.int32, (GROUP, GROUP), 0)
        col = lax.broadcasted_iota(jnp.int32, (GROUP, GROUP), 1)
        upto = (col <= row) & (col // TOK == row // TOK)
        upto_ref[...] = upto.astype(jnp.float32).astype(jnp.bfloat16)
        slot = lax.broadcasted_iota(jnp.int32, (2 * SLOTS, GROUP), 0)
        token = lax.broadcasted_iota(jnp.int32, (2 * SLOTS, GROUP), 1)
        want_ref[...] = place_of(slot, token).astype(jnp.float32)
        token = lax.broadcasted_iota(jnp.int32, (GROUP, 2 * SLOTS), 0)
        slot = lax.broadcasted_iota(jnp.int32, (GROUP, 2 * SLOTS), 1)
        wanted_ref[...] = place_of(slot, token).astype(jnp.float32)

    high, low = slot_tables(ids)
    table = high.astype(jnp.float32).astype(jnp.bfloat16)

    @pl.loop(0, x_ref.shape[0] // GROUP)
    def _(g):
        tokens = pl.ds(pl.multiple_of(g * GROUP, GROUP), GROUP)
        mine = pl.ds(pl.multiple_of(g * SLOTS, 16), SLOTS)
        gates = x_ref[tokens, width : width + GATE_LANES]
        hit = (gates.astype(jnp.float32) != 0.0).astype(jnp.float32)
        count = jnp.dot(
            upto_ref[...], hit.astype(jnp.bfloat16), preferred_element_type=jnp.float32
        )
        count = (count * hit).astype(jnp.bfloat16)
        by_slot = lax.dot_general(table, count, across, preferred_element_type=jnp.float32)
        pick = (by_slot == want_ref[...]).astype(jnp.float32).astype(jnp.bfloat16)
        by_token = lax.dot_general(count, table, across, preferred_element_type=jnp.float32)
        put = (by_token == wanted_ref[...]).astype(jnp.float32)
        st_ref[g] = put.astype(jnp.bfloat16)
        for n in range(width // tile):
            cols = slice(n * tile, (n + 1) * tile)
            rows = jnp.dot(pick, x_ref[tokens, cols], preferred_element_type=jnp.float32)
            rows = rows.astype(jnp.bfloat16)
            rows_ref[0, mine, cols] = rows[:SLOTS]
            rows_ref[1, mine, cols] = rows[SLOTS:]
        picked = jnp.dot(pick, gates, preferred_element_type=jnp.float32)
        picked = jnp.where(high | low, picked, 0.0)
        gate_ref[0, mine] = picked[:SLOTS]
        gate_ref[1, mine] = picked[SLOTS:]


def pick_call(ids, gathered, width):
    groups = gathered.shape[0] // GROUP
    step = 2
    return pl.pallas_call(
        pick_kernel,
        out_shape=(
            jax.ShapeDtypeStruct((2, groups * SLOTS, width), jnp.bfloat16),
            jax.ShapeDtypeStruct((2, groups * SLOTS, GATE_LANES), jnp.float32),
            jax.ShapeDtypeStruct((groups, GROUP, 2 * SLOTS), jnp.bfloat16),
        ),
        grid_spec=pltpu.PrefetchScalarGridSpec(
            num_scalar_prefetch=1,
            grid=(groups // step,),
            in_specs=[pl.BlockSpec((step * GROUP, width + GATE_LANES), lambda g, ids: (g, 0))],
            out_specs=(
                pl.BlockSpec((2, step * SLOTS, width), lambda g, ids: (0, g, 0)),
                pl.BlockSpec((2, step * SLOTS, GATE_LANES), lambda g, ids: (0, g, 0)),
                pl.BlockSpec((step, GROUP, 2 * SLOTS), lambda g, ids: (g, 0, 0)),
            ),
            scratch_shapes=[
                pltpu.VMEM((GROUP, GROUP), jnp.bfloat16),
                pltpu.VMEM((2 * SLOTS, GROUP), jnp.float32),
                pltpu.VMEM((GROUP, 2 * SLOTS), jnp.float32),
            ],
        ),
        compiler_params=pltpu.CompilerParams(
            dimension_semantics=("arbitrary",), vmem_limit_bytes=26 << 20
        ),
        cost_estimate=pl.CostEstimate(
            flops=4 * groups * SLOTS * GROUP * width,
            bytes_accessed=4 * groups * GROUP * width,
            transcendentals=0,
        ),
        name="pick",
    )(ids, gathered)


def put_kernel(widths, plane, st_ref, y0_ref, y1_ref, *outs):
    columns = y0_ref.shape[-1]
    tile = min(256, columns)
    cuts = widths or (tile,) * (columns // tile)

    @pl.loop(0, RING)
    def _(g):
        mine = pl.ds(pl.multiple_of(g * SLOTS, 16), SLOTS)
        for n, cut in enumerate(cuts):
            cols = slice(sum(cuts[:n]), sum(cuts[: n + 1]))
            y = jnp.concatenate([y0_ref[mine, cols], y1_ref[mine, cols]], axis=0)
            out = jnp.dot(st_ref[g], y, preferred_element_type=jnp.float32)
            out = out.astype(jnp.bfloat16)
            if widths:
                outs[n][0, pl.ds(pl.multiple_of(g * GROUP, GROUP), GROUP), :] = out
            else:
                for b in range(RING):
                    outs[0][g * RING + b, 0, :, cols] = out[b * TOK : (b + 1) * TOK]


def put_call(plane, chosen, y0, y1, widths=()):
    groups = chosen.shape[0]
    columns = y0.shape[-1]
    turns = (lambda z, plane: ((plane[0] + 3 - z) & 3, 0, 0)), (
        lambda z, plane: ((z + 3 - plane[0]) & 3, 0, 0)
    )
    if widths:
        out_shape = tuple(
            jax.ShapeDtypeStruct((RING, RING * GROUP, cut), jnp.bfloat16) for cut in widths
        )
        out_specs = tuple(
            pl.BlockSpec((1, RING * GROUP, cut), turns[n % 2]) for n, cut in enumerate(widths)
        )
    else:
        out_shape = jax.ShapeDtypeStruct((RING * RING, RING, TOK, columns), jnp.bfloat16)
        out_specs = pl.BlockSpec(
            (RING * RING, 1, TOK, columns), lambda z, plane: (0, (z + RING - plane[0]) & 3, 0, 0)
        )
    rows = pl.BlockSpec((RING * SLOTS, columns), lambda z, plane: (z, 0))
    return pl.pallas_call(
        functools.partial(put_kernel, widths),
        out_shape=out_shape,
        grid_spec=pltpu.PrefetchScalarGridSpec(
            num_scalar_prefetch=1,
            grid=(groups // RING,),
            in_specs=[
                pl.BlockSpec((RING, GROUP, 2 * SLOTS), lambda z, plane: (z, 0, 0)), rows, rows,
            ],
            out_specs=out_specs,
        ),
        compiler_params=pltpu.CompilerParams(
            dimension_semantics=("arbitrary",), vmem_limit_bytes=26 << 20
        ),
        cost_estimate=pl.CostEstimate(
            flops=4 * groups * GROUP * SLOTS * columns,
            bytes_accessed=3 * groups * GROUP * columns,
            transcendentals=0,
        ),
        name="put_halves" if widths else "put",
    )(plane, chosen, y0, y1)


def run_hidden(rows, gate, w_gate, w_up):
    gate = jnp.sum(gate, axis=1, keepdims=True)
    gate_part = jnp.dot(rows, w_gate, preferred_element_type=jnp.float32)
    up_part = jnp.dot(rows, w_up, preferred_element_type=jnp.float32)
    return (jax.nn.silu(gate_part) * up_part * gate).astype(jnp.bfloat16)


def run_down(hidden, down_weights):
    return [
        jnp.dot(h, w, preferred_element_type=jnp.float32).astype(jnp.bfloat16)
        for h, w in zip(hidden, down_weights)
    ]


def add_rounded(a, b):
    return (a.astype(jnp.float32) + b.astype(jnp.float32)).astype(jnp.bfloat16)


def body(
    streams, phi_matrix, mix_scale, mix_bias, router, expert_index_table, w_gate, w_up, down_weight
):
    width, ff = w_gate.shape[1], w_gate.shape[2]
    swap = [(0, 1), (1, 0)]
    own = (w_gate[0], w_up[0], down_weight[0])
    other = tuple(lax.ppermute(w, "c", swap) for w in own)
    pre, post, mixing = mix_coefficients(streams, phi_matrix, mix_scale, mix_bias)
    layer_in = mix_input(streams, pre)
    gates = dense_gates(layer_in, router, expert_index_table)
    packed = jnp.concatenate([layer_in, gates], axis=1)
    gathered = lax.all_gather(packed, ("z", "y", "x"), axis=0, tiled=True)
    core = lax.axis_index("c")
    pair = 2 * (lax.axis_index("y") * RING + lax.axis_index("x"))
    ids = jnp.stack([pair + core, pair + 1 - core]).astype(jnp.int32)
    plane = lax.axis_index("z")
    planes = plane.reshape(1).astype(jnp.int32)
    late = width - sum(CHUNKS)
    downs = (own[2], other[2])
    late_downs, early_downs = [w[:, :late] for w in downs], [w[:, late:] for w in downs]
    gathered, late_downs, early_downs = lax.optimization_barrier(
        (gathered, late_downs, early_downs)
    )
    rows, gate, chosen = pick_call(ids, gathered, width)
    hidden = [run_hidden(rows[e], gate[e], *w[:2]) for e, w in enumerate((own, other))]
    hidden = lax.optimization_barrier(hidden)
    dense = put_call(planes, chosen, *run_down(hidden, late_downs))
    summed = lax.psum_scatter(
        dense.reshape(-1, late), ("y", "x"), scatter_dimension=0, tiled=True
    ).reshape(RING, TOK, late)
    widths = tuple(cut // 2 for cut in CHUNKS for way in range(2))
    halves = put_call(planes, chosen, *run_down(hidden, early_downs), widths)
    travel = [half[0] for half in halves]
    for stop in range(1, RING):
        for part in range(len(widths)):
            turn = (1, RING - 1)[part % 2]
            ring = [(i, (i + turn) % RING) for i in range(RING)]
            travel[part] = add_rounded(lax.ppermute(travel[part], "z", ring), halves[part][stop])
    early_out = []
    for chunk, cut in enumerate(CHUNKS):
        shares = jnp.concatenate(travel[2 * chunk : 2 * chunk + 2], axis=1)
        shares = shares.reshape(RING * RING, TOK, cut)
        shares = lax.all_to_all(shares, ("y", "x"), split_axis=0, concat_axis=0, tiled=True)
        early_out.append(jnp.sum(shares.astype(jnp.float32), axis=0))
    late_out = summed[0].astype(jnp.float32)
    for shift in range(1, RING):
        ring = [(i, (i + shift) % RING) for i in range(RING)]
        late_out = late_out + lax.ppermute(summed[shift], "z", ring).astype(jnp.float32)
    moe_out = jnp.concatenate([late_out] + early_out, axis=1)
    return mix_output(streams, mixing, post, moe_out)


def solution(mesh):
    torus = Mesh(mesh.devices.reshape(RING, RING, RING, 2), ("z", "y", "x", "c"))
    tokens, experts = ("z", "y", "x", "c"), ("y", "x", "c")
    in_specs = (
        P(tokens, None, None),
        P(),
        P(),
        P(),
        P(),
        P(tokens, None),
        P(experts, None, "z"),
        P(experts, None, "z"),
        P(experts, "z", None),
    )
    out_specs = P(tokens, None, None)
    return jax.shard_map(
        body, mesh=torus, in_specs=in_specs, out_specs=out_specs, check_vma=False
    )
```
